256 devices in a mesh: row: 4 (over x), col: 16 (over z, core), depth: 4 (over y).
Axes of the slice: x: 4, y: 4, z: 8, core: 2. Of those that a mesh axis runs over, the one named last changes fastest.
Arguments:
- amplitudes: float32 [8, 768, 6144], P('depth', 'col', 'row'), may hold values from -6 to 6
- integrals: float32 [8, 768, 16, 768], P('depth', 'row', 'col'), may hold values from -0.21875 to 0.21875
- irrep_virtual: int32 [768], replicated, may hold values from 0 to 7, as said below
- irrep_first: int32 [8], replicated, may hold values from 0 to 7
- irrep_second: int32 [8], replicated, may hold values from 0 to 7
- irrep_target: int32 [16], replicated, may hold values from 0 to 7
Outputs:
- cycle_term: float32 [16, 768, 6144], P('col', 'depth', 'row')
The draws below stay inside these ranges and needn't reach their ends.
Inputs may be any that keep to these rules, and one draw needn't show every extreme that they name: `irrep_virtual`: labels never fall along the virtual orbitals, so each irrep is one contiguous block, the blocks in rising order of irrep; every irrep holds 64 or more virtuals.
All inputs are finite; a program needn't handle non-finite values.
Results may differ from the reference program's by a relative error of at most 0.0001.
Values sent between devices are 32-bit elements; how exact they have to be, the bound alone decides.
No kernel may reach another device: no remote copies, remote signals or barrier semaphores. Data moves between devices by JAX's collectives and lax.ppermute only.
A program may use at most 64 MiB of HBM per device.

```python
import jax
import jax.numpy as jnp
from jax import lax

V = 768
OI = 8
OK = 8
OJ = 16


def draw_irrep_virtual(key, part):
    least_size = V // 12
    spare_count = V - 8 * least_size
    chosen = jax.random.randint(key, (spare_count,), 0, 8)
    counts = jnp.sum((chosen[:, None] == jnp.arange(8)[None, :]).astype(jnp.int32), axis=0)
    bounds = jnp.cumsum(least_size + counts).astype(jnp.int32)
    places = jnp.arange(V, dtype=jnp.int32)
    return jnp.sum((places[:, None] >= bounds[None, :]).astype(jnp.int32), axis=1).astype(jnp.int32)


def plant(entries, own_key, low, top_value):
    extent = entries.shape
    index_at = [jax.random.randint(jax.random.fold_in(own_key, axis), (), 0, extent[axis]) for axis in range(len(extent))]
    entries = entries.at[tuple(index_at)].set(low)
    longest = extent.index(max(extent))
    index_at[longest] = (index_at[longest] + 1) % extent[longest]
    return entries.at[tuple(index_at)].set(top_value)


def shard_levels(key, shape, shards, smallest, high):
    loudness, own = 1.0, jax.random.fold_in(key, 6)
    for position, shards_of in shards:
        heights = jnp.exp(jax.random.uniform(jax.random.fold_in(own, position), (shards_of,), jnp.float32, smallest / len(shards), high / len(shards)))
        loudness = loudness * jnp.repeat(heights, shape[position] // shards_of).reshape([-1 if axis == position else 1 for axis in range(len(shape))])
    return loudness


def scatter_about(stream_key, dims, scale, limit, cuts=(), kind=jnp.bfloat16):
    entries = jax.random.normal(stream_key, dims, jnp.float32) * scale
    if len(cuts) > 0:
        entries = shard_levels(stream_key, dims, cuts, -0.22, 0.18) * entries
    return jnp.clip(entries, min=-limit, max=limit).astype(kind)


def setup_inputs(seed: int = 0) -> dict:
    keys = jax.random.split(jax.random.key(seed), 7)
    return {
        "amplitudes": scatter_about(keys[0], (OK, V, V * OI), 1.0, 6.0, ((0, 4), (1, 16), (2, 4)), jnp.float32),
        "integrals": scatter_about(keys[1], (OK, V, OJ, V), (OK * V // 8) ** -0.5, 0.21875, ((0, 4), (1, 4), (2, 16)), jnp.float32),
        "irrep_virtual": draw_irrep_virtual(jax.random.fold_in(keys[6], 71), 0),
        "irrep_first": plant(jax.random.randint(keys[3], (OI,), 0, 8), jax.random.fold_in(keys[3], 1), 0, 7).astype(jnp.int32),
        "irrep_second": plant(jax.random.randint(keys[4], (OK,), 0, 8), jax.random.fold_in(keys[4], 1), 0, 7).astype(jnp.int32),
        "irrep_target": plant(jax.random.randint(keys[5], (OJ,), 0, 8), jax.random.fold_in(keys[5], 1), 0, 7).astype(jnp.int32),
    }


def merged_labels(irrep_virtual, irrep_first):
    return jnp.bitwise_xor(irrep_virtual[:, None], irrep_first[None, :]).reshape(-1).astype(jnp.int32)


def reference(amplitudes, integrals, irrep_virtual, irrep_first, irrep_second, irrep_target):
    labels_x = merged_labels(irrep_virtual, irrep_first)
    cycle_term = jnp.zeros((OJ, V, V * OI), jnp.float32)
    for orbital in range(OK):
        label_k = irrep_second[orbital]
        left_mask = (jnp.bitwise_xor(jnp.bitwise_xor(label_k, irrep_virtual)[:, None], labels_x[None, :]) == 0).astype(jnp.float32)
        masked_amp = amplitudes[orbital] * left_mask
        parity = jnp.bitwise_xor(
            jnp.bitwise_xor(label_k, irrep_virtual)[:, None, None],
            jnp.bitwise_xor(irrep_target[:, None], irrep_virtual[None, :])[None, :, :])
        masked_int = integrals[orbital] * (parity == 0).astype(jnp.float32)
        cycle_term = cycle_term + jnp.einsum("cjb,cx->jbx", masked_int, masked_amp,
                                           precision=lax.Precision.HIGHEST, preferred_element_type=jnp.float32)
    return cycle_term
```

```python
import functools

import jax
import jax.numpy as jnp
from jax import lax
from jax.experimental import pallas as pl
from jax.experimental.pallas import tpu as pltpu
from jax.sharding import PartitionSpec as P

LANES = 512
BLOCK = 128
SMEM = pl.BlockSpec(memory_space=pltpu.SMEM)
VMEM = pl.BlockSpec(memory_space=pltpu.VMEM)
ANY = pl.BlockSpec(memory_space=pl.ANY)
F32, BF16, I32 = jnp.float32, jnp.bfloat16, jnp.int32


def label_of(place, starts):
    label = jnp.zeros_like(place)
    for irrep in range(1, 8):
        label = label + (place >= starts[irrep]).astype(I32)
    return label


def choose(index, scalars):
    out = jnp.full_like(index, scalars[0])
    for n in range(1, len(scalars)):
        out = jnp.where(index == n, scalars[n], out)
    return out


def two_terms(x):
    high = x.astype(BF16)
    return high, (x - high.astype(F32)).astype(BF16)


def nt(a, b):
    return lax.dot_general(a, b, (((1,), (1,)), ((), ())), preferred_element_type=F32)


def tn(a, b):
    return lax.dot_general(a, b, (((0,), (0,)), ((), ())), preferred_element_type=F32)


def x_places(pos, starts, first, x_local, oi):
    a_local = x_local // oi
    base = pos[0] * a_local
    x = lax.broadcasted_iota(I32, (1, x_local), 1)
    i = x % oi
    a = base + x // oi
    label = label_of(a, starts)
    firsts = [first[n] for n in range(oi)]
    s = label ^ choose(i, firsts)
    low = [jnp.maximum(starts[n], base) for n in range(8)]
    count = [jnp.maximum(jnp.minimum(starts[n + 1], base + a_local) - low[n], 0) for n in range(8)]
    place = a - choose(label, low)
    for n in range(oi - 1):
        place = place + jnp.where(n < i, choose(s ^ firsts[n], count), 0)
    return s, place - pos[3] * LANES


def pack_t_kernel(pos, starts, first, second, t_ref, out_ref, g_ref, s_ref):
    k_local, c_local, x_local = t_ref.shape
    s, place = x_places(pos, starts, first, x_local, first.shape[0])
    s_ref[...] = jnp.broadcast_to(s, s_ref.shape)
    for n in range(LANES // 128):
        rows = n * 128 + lax.broadcasted_iota(I32, (128, x_local), 0)
        g_ref[n * 128 : n * 128 + 128, :] = jnp.where(rows == place, 1.0, 0.0).astype(BF16)
    c = pos[1] * c_local + lax.broadcasted_iota(I32, (c_local, 1), 0)
    label = label_of(c, starts)
    parts = []
    for k in range(k_local):
        keep = (label ^ second[pos[2] * k_local + k]) == s
        parts.extend(two_terms(jnp.where(keep, t_ref[k], 0.0)))
    packed = nt(jnp.concatenate(parts, 0), g_ref[...])
    for k in range(k_local):
        n = 2 * k * c_local
        out_ref[k] = packed[n : n + c_local] + packed[n + c_local : n + 2 * c_local]


def pack_w_kernel(pos, starts, second, target, w_ref, out_ref):
    k_local, c_local, _ = out_ref.shape
    rows = k_local * c_local
    tiles = w_ref.shape[0] // rows
    row = lax.broadcasted_iota(I32, (c_local, 1), 0)
    label = label_of(pos[0] * c_local + row, starts) ^ target[pos[1]]
    wanted = jnp.concatenate([label ^ second[pos[2] * k_local + k] for k in range(k_local)], 0)
    firsts = [starts[n] // 8 * 8 for n in range(8)]
    total = jnp.zeros((2 * rows, BLOCK), F32)
    for q in range(tiles):
        b = q * 128 + lax.broadcasted_iota(I32, (1, 128), 1)
        label_b = label_of(b, starts)
        place = b - choose(label_b, firsts) - pos[4] * BLOCK
        hot = jnp.where(lax.broadcasted_iota(I32, (BLOCK, 128), 0) == place, 1.0, 0.0).astype(BF16)
        w = jnp.where(wanted == label_b, w_ref[pl.ds(q, rows, stride=tiles), :], 0.0)
        total = total + nt(jnp.concatenate(two_terms(w), 0), hot)
    for k in range(k_local):
        out_ref[k] = total[k * c_local : (k + 1) * c_local] + total[rows + k * c_local : rows + (k + 1) * c_local]


def product_kernel(plan, *refs):
    pos, starts, second, target = refs[:4]
    pieces = refs[4 : 4 + len(plan)]
    outs = refs[4 + len(plan) : 8 + len(plan)]
    t_all, w_all, total, sems = refs[8 + len(plan) :]
    k_local, c_all, _ = t_all.shape
    b_local = outs[0].shape[0]
    copies = []
    for n, (kind, k, shift, piece) in enumerate(zip(*zip(*plan), pieces)):
        size = piece.shape[-2]
        into = t_all if kind == "t" else w_all
        if kind == "t":
            chip = lax.rem(pos[1] // 2 + shift[0] + 8, 8)
            at = (chip * 2 + (pos[1] % 2 if shift[1] == 0 else 1 - pos[1] % 2)) * size
        else:
            at = lax.rem(pos[0] + shift + 4, 4) * size
        at = pl.multiple_of(at, 8)
        if k is None:
            copy = pltpu.make_async_copy(piece, into.at[:, pl.ds(at, size), :], sems.at[n])
        else:
            copy = pltpu.make_async_copy(piece, into.at[pl.ds(k, 1), pl.ds(at, size), :], sems.at[n])
        copy.start()
        copies.append(copy)
    total[...] = jnp.zeros_like(total)
    for copy in copies:
        copy.wait()
    row = lax.broadcasted_iota(I32, (128, 1), 0)
    for irrep in range(8):
        s = target[pos[1]] ^ irrep
        sums = jnp.zeros((BLOCK, LANES), F32)
        for k in range(k_local):
            p = s ^ second[pos[2] * k_local + k]
            begin, end = starts[p], starts[p + 1]
            aligned = begin // 8 * 8

            def step(n, acc, k=k, begin=begin, end=end, aligned=aligned):
                nominal = aligned + n * 128
                at = pl.multiple_of(jnp.minimum(nominal, c_all - 128), 8)
                c = at + row
                keep = (c >= jnp.maximum(begin, nominal)) & (c < end)
                w_high, w_low = two_terms(jnp.where(keep, w_all[k, pl.ds(at, 128), :], 0.0))
                t_high, t_low = two_terms(t_all[k, pl.ds(at, 128), :])
                return acc + tn(w_high, t_high) + tn(w_high, t_low) + tn(w_low, t_high)

            sums = lax.fori_loop(0, (end - aligned + 127) // 128, step, sums)
        at = starts[irrep] // 8 * 8 + pos[4] * BLOCK

        @pl.when(at < starts[irrep + 1])
        def _(at=pl.multiple_of(at, 8), sums=sums):
            total[pl.ds(at, BLOCK), :] += sums

    copies = []
    for n, out in enumerate(outs):
        at = pl.multiple_of(lax.rem(pos[2] + n, 4) * b_local, 8)
        copy = pltpu.make_async_copy(total.at[pl.ds(at, b_local), :], out, sems.at[n])
        copy.start()
        copies.append(copy)
    for copy in copies:
        copy.wait()


def expand_kernel(pos, starts, target, g_ref, s_ref, *refs):
    out_ref = refs[-1]
    b_local = refs[0].shape[0]
    sums = refs[0][...] + refs[1][...] + (refs[2][...] + refs[3][...])
    both = jnp.dot(jnp.concatenate(two_terms(sums), 0), g_ref[...], preferred_element_type=F32)
    b = pos[2] * b_local + lax.broadcasted_iota(I32, (b_local, 1), 0)
    keep = (label_of(b, starts) ^ target[pos[1]]) == s_ref[:1, :]
    value = jnp.where(keep, both[:b_local] + both[b_local:], 0.0)
    out_ref[0] = value + refs[4][0] if len(refs) > 5 else value


def params():
    return pltpu.CompilerParams(vmem_limit_bytes=48 * 1024 * 1024)


def one_pass(pos, starts, first, second, target, amplitudes, integrals, before):
    k_local, c_local, x_local = amplitudes.shape
    w_rows = integrals.shape[1]
    v = integrals.shape[3]
    b_local = v // 4
    shape = jax.ShapeDtypeStruct
    t0, hot, s_of = pl.pallas_call(
        pack_t_kernel,
        out_shape=(shape((k_local, c_local, LANES), F32), shape((LANES, x_local), BF16), shape((8, x_local), I32)),
        in_specs=[SMEM] * 4 + [VMEM],
        out_specs=(VMEM,) * 3,
        compiler_params=params(),
        name="pack_t",
    )(pos, starts, first, second, amplitudes)
    w0 = pl.pallas_call(
        pack_w_kernel,
        out_shape=shape((k_local, w_rows, BLOCK), F32),
        in_specs=[SMEM] * 4 + [VMEM],
        out_specs=VMEM,
        compiler_params=params(),
        name="pack_w",
    )(pos, starts, second, target, integrals.reshape(k_local * w_rows * (v // 128), 128))

    def along(x, axis, n, step):
        return lax.ppermute(x, axis, [(i, (i + step) % n) for i in range(n)])

    def swap(x):
        return lax.ppermute(x, "col", [(i, i ^ 1) for i in range(16)])

    got = [(None, (0, 0), t0)]
    right = left = t0
    for n in range(1, 4):
        right, left = along(right, "col", 16, 2), along(left, "col", 16, -2)
        got += [(None, (-n, 0), right), (None, (n, 0), left)]
    got += [(0, (4, 0), along(right[:1], "col", 16, 2)), (1, (4, 0), along(left[1:], "col", 16, -2))]
    got += [(k, (shift[0], 1), swap(piece)) for k, shift, piece in got]
    plan = [("t", k, shift) for k, shift, _ in got]
    pieces = [piece for _, _, piece in got]
    plan += [("w", None, -n) for n in range(4)]
    pieces += [w0] + [along(w0, "row", 4, n) for n in range(1, 4)]
    sums = pl.pallas_call(
        functools.partial(product_kernel, plan),
        out_shape=(shape((b_local, LANES), F32),) * 4,
        in_specs=[SMEM] * 4 + [ANY] * len(pieces),
        out_specs=(ANY,) * 4,
        scratch_shapes=[
            pltpu.VMEM((k_local, v, LANES), F32),
            pltpu.VMEM((k_local, v, BLOCK), F32),
            pltpu.VMEM((v + BLOCK, LANES), F32),
            pltpu.SemaphoreType.DMA((len(pieces),)),
        ],
        compiler_params=params(),
        name="product",
    )(pos, starts, second, target, *pieces)
    sums = [sums[0]] + [along(sums[n], "depth", 4, n) for n in range(1, 4)]
    more = [] if before is None else [before]
    return pl.pallas_call(
        expand_kernel,
        out_shape=shape((1, b_local, x_local), F32),
        in_specs=[SMEM] * 3 + [VMEM] * (6 + len(more)),
        out_specs=VMEM,
        compiler_params=params(),
        name="expand",
    )(pos, starts, target, hot, s_of, *sums, *more)


def per_device(amplitudes, integrals, irrep_virtual, irrep_first, irrep_second, irrep_target):
    v = irrep_virtual.shape[0]
    a_local = amplitudes.shape[2] // irrep_first.shape[0]
    starts = jnp.sum((irrep_virtual[None, :] < jnp.arange(16, dtype=I32)[:, None]).astype(I32), axis=1)
    where = [lax.axis_index(n).astype(I32) for n in ("row", "col", "depth")]

    def position(n_lane, n_block):
        return jnp.stack(where + [n_lane, n_block, 0, 0, 0]).astype(I32)

    def run(n_lane, n_block, before):
        return one_pass(
            position(n_lane, n_block), starts, irrep_first, irrep_second, irrep_target, amplitudes, integrals, before
        )

    out = run(jnp.int32(0), jnp.int32(0), None)
    edges = jnp.arange(0, v, a_local, dtype=I32)
    low, high = starts[:8], starts[1:9]
    count = jnp.maximum(jnp.minimum(high, edges[:, None] + a_local) - jnp.maximum(low, edges[:, None]), 0)
    same = (jnp.arange(8)[:, None, None] ^ irrep_first[None, None, :]) == jnp.arange(8)[None, :, None]
    most = jnp.max(jnp.sum(count[:, None, :, None] * same[None].astype(I32), axis=(2, 3)))
    n_lanes = (most + LANES - 1) // LANES
    n_blocks = (jnp.max(high - low // 8 * 8) + BLOCK - 1) // BLOCK
    return lax.fori_loop(1, n_lanes * n_blocks, lambda n, acc: run(n % n_lanes, n // n_lanes, acc), out)


def solution(mesh):
    return jax.shard_map(
        per_device,
        mesh=mesh,
        in_specs=(P("depth", "col", "row"), P("depth", "row", "col", None), P(), P(), P(), P()),
        out_specs=P("col", "depth", "row"),
        check_vma=False,
    )
```

```python
import functools

import jax
import jax.numpy as jnp
from jax import lax
from jax.experimental import pallas as pl
from jax.experimental.pallas import tpu as pltpu
from jax.sharding import PartitionSpec as P


LANES = 512
BLOCK = 128
SMEM = pl.BlockSpec(memory_space=pltpu.SMEM)
VMEM = pl.BlockSpec(memory_space=pltpu.VMEM)
ANY = pl.BlockSpec(memory_space=pl.ANY)
F32, BF16, I32 = jnp.float32, jnp.bfloat16, jnp.int32


def label_of(place, starts):
    label = jnp.zeros_like(place)
    for irrep in range(1, 8):
        label = label + (place >= starts[irrep]).astype(I32)
    return label


def choose(index, scalars):
    out = jnp.full_like(index, scalars[0])
    for n in range(1, len(scalars)):
        out = jnp.where(index == n, scalars[n], out)
    return out


def two_terms(x):
    high = x.astype(BF16)
    return high, (x - high.astype(F32)).astype(BF16)


def nt(a, b):
    return lax.dot_general(a, b, (((1,), (1,)), ((), ())), preferred_element_type=F32)


def tn(a, b):
    return lax.dot_general(a, b, (((0,), (0,)), ((), ())), preferred_element_type=F32)


def x_places(pos, starts, first, x_local, oi):
    a_local = x_local // oi
    base = pos[0] * a_local
    x = lax.broadcasted_iota(I32, (1, x_local), 1)
    i = x % oi
    a = base + x // oi
    label = label_of(a, starts)
    firsts = [first[n] for n in range(oi)]
    s = label ^ choose(i, firsts)
    low = [jnp.maximum(starts[n], base) for n in range(8)]
    count = [jnp.maximum(jnp.minimum(starts[n + 1], base + a_local) - low[n], 0) for n in range(8)]
    place = a - choose(label, low)
    for n in range(oi - 1):
        place = place + jnp.where(n < i, choose(s ^ firsts[n], count), 0)
    return s, place - pos[3] * LANES


def pack_t_kernel(pos, starts, first, second, t_ref, out_ref, g_ref):
    k_local, c_local, x_local = t_ref.shape
    s, place = x_places(pos, starts, first, x_local, first.shape[0])
    c = pos[1] * c_local + lax.broadcasted_iota(I32, (c_local, 1), 0)
    label = label_of(c, starts)
    parts = []
    for k in range(k_local):
        keep = (label ^ second[pos[2] * k_local + k]) == s
        parts.extend(two_terms(jnp.where(keep, t_ref[k], 0.0)))
    stacked = jnp.concatenate(parts, 0)
    for n in range(LANES // 128):
        lanes = slice(n * 128, n * 128 + 128)
        rows = n * 128 + lax.broadcasted_iota(I32, (128, x_local), 0)
        hot = jnp.where(rows == place, 1.0, 0.0).astype(BF16)
        g_ref[lanes, :] = hot
        packed = nt(stacked, hot)
        for k in range(k_local):
            at = 2 * k * c_local
            out_ref[k, :, lanes] = packed[at : at + c_local] + packed[at + c_local : at + 2 * c_local]


def pack_w_kernel(pos, starts, second, target, w_ref, out_ref):
    k_local, c_local, _ = out_ref.shape
    rows = k_local * c_local
    tiles = w_ref.shape[0] // rows
    row = lax.broadcasted_iota(I32, (c_local, 1), 0)
    label = label_of(pos[0] * c_local + row, starts) ^ target[pos[1]]
    wanted = jnp.concatenate([label ^ second[pos[2] * k_local + k] for k in range(k_local)], 0)
    firsts = [starts[n] // 8 * 8 for n in range(8)]
    total = jnp.zeros((2 * rows, BLOCK), F32)
    for q in range(tiles):
        b = q * 128 + lax.broadcasted_iota(I32, (1, 128), 1)
        label_b = label_of(b, starts)
        place = b - choose(label_b, firsts) - pos[4] * BLOCK
        hot = jnp.where(lax.broadcasted_iota(I32, (BLOCK, 128), 0) == place, 1.0, 0.0).astype(BF16)
        w = jnp.where(wanted == label_b, w_ref[pl.ds(q, rows, stride=tiles), :], 0.0)
        total = total + nt(jnp.concatenate(two_terms(w), 0), hot)
    for k in range(k_local):
        out_ref[k] = total[k * c_local : (k + 1) * c_local] + total[rows + k * c_local : rows + (k + 1) * c_local]


def place_piece(pos, kind, shift, size):
    if kind == "t":
        chip = lax.rem(pos[1] // 2 + shift[0] + 8, 8)
        at = (chip * 2 + (pos[1] % 2 if shift[1] == 0 else 1 - pos[1] % 2)) * size
    else:
        at = lax.rem(pos[0] + shift + 4, 4) * size
    return pl.multiple_of(at, 8)


def stacks(w, t):
    w_high, w_low = two_terms(w)
    t_high, t_low = two_terms(t)
    return [w_high, w_high, w_low], [t_high, t_low, t_high]


def early_kernel(plan, *refs):
    pos, starts, second, target = refs[:4]
    pieces = refs[4 : 4 + len(plan)]
    total, w_out, t_all, w_all, sems = refs[4 + len(plan) :]
    k_local, c_all, _ = t_all.shape
    copies = []
    for n, (kind, shift, piece) in enumerate(zip(*zip(*plan), pieces)):
        size = piece.shape[-2]
        into = t_all if kind == "t" else w_all
        at = place_piece(pos, kind, shift, size)
        copies.append(pltpu.make_async_copy(piece, into.at[:, pl.ds(at, size), :], sems.at[n]))
        copies[-1].start()
    missing = c_all // 8
    at = pl.multiple_of(lax.rem(pos[1] // 2 + 4, 8) * missing, 8)
    for k in range(k_local):
        t_all[k, pl.ds(at, missing), :] = jnp.zeros((missing, LANES), F32)
    total[...] = jnp.zeros_like(total)
    for copy in copies:
        copy.wait()
    late = pl.ds(at, missing)
    w_out[...] = w_all[:, late, :]
    row = lax.broadcasted_iota(I32, (128, 1), 0)

    def one_irrep(irrep, _):
        s = target[pos[1]] ^ irrep
        spans = []
        for k in range(k_local):
            p = s ^ second[pos[2] * k_local + k]
            spans.append((starts[p], starts[p + 1], starts[p] // 8 * 8))
        trips = [(end - aligned + 127) // 128 for _, end, aligned in spans]

        def step(n, acc):
            ws, ts = [], []
            for k, (begin, end, aligned) in enumerate(spans):
                nominal = aligned + n * 128
                at = pl.multiple_of(jnp.minimum(nominal, c_all - 128), 8)
                c = at + row
                keep = (c >= jnp.maximum(begin, nominal)) & (c < end)
                w, t = stacks(jnp.where(keep, w_all[k, pl.ds(at, 128), :], 0.0), t_all[k, pl.ds(at, 128), :])
                ws, ts = ws + w, ts + t
            return acc + tn(jnp.concatenate(ws, 0), jnp.concatenate(ts, 0))

        sums = lax.fori_loop(0, jnp.maximum(*trips), step, jnp.zeros((BLOCK, LANES), F32))
        to = starts[irrep] // 8 * 8 + pos[4] * BLOCK

        @pl.when(to < starts[irrep + 1])
        def _():
            total[pl.ds(pl.multiple_of(to, 8), BLOCK), :] += sums

        return 0

    lax.fori_loop(0, 8, one_irrep, 0)


def late_kernel(pos, starts, second, target, total, w, t0, t1, u0, u1, *refs):
    outs, (t_all, sums, sems) = refs[:-3], refs[-3:]
    half = t0.shape[1]
    c_late = 2 * half
    copies = []
    for n, (k, shift, piece) in enumerate(((0, 0, t0), (1, 0, t1), (0, 1, u0), (1, 1, u1))):
        at = pl.multiple_of((pos[1] % 2 if shift == 0 else 1 - pos[1] % 2) * half, 8)
        copies.append(pltpu.make_async_copy(piece, t_all.at[pl.ds(k, 1), pl.ds(at, half), :], sems.at[n]))
        copies[-1].start()
    whole = pltpu.make_async_copy(total, sums, sems.at[4])
    whole.start()
    for copy in copies:
        copy.wait()
    whole.wait()
    base = lax.rem(pos[1] // 2 + 4, 8) * c_late
    c = base + lax.broadcasted_iota(I32, (c_late, 1), 0)
    label = label_of(c, starts)
    first_p = last_p = 0
    for irrep in range(1, 8):
        first_p = first_p + (base >= starts[irrep]).astype(I32)
        last_p = last_p + (base + c_late - 1 >= starts[irrep]).astype(I32)

    def one_p(p, _):
        for k in range(2):
            irrep = p ^ second[pos[2] * 2 + k] ^ target[pos[1]]
            ws, ts = stacks(jnp.where(label == p, w[k], 0.0), t_all[k])
            term = tn(jnp.concatenate(ws, 0), jnp.concatenate(ts, 0))
            to = starts[irrep] // 8 * 8 + pos[4] * BLOCK

            @pl.when(to < starts[irrep + 1])
            def _(term=term, to=to):
                sums[pl.ds(pl.multiple_of(to, 8), BLOCK), :] += term

        return 0

    lax.fori_loop(first_p, last_p + 1, one_p, 0)
    b_local = outs[-1].shape[0]
    copies = []
    for n, (step, skip) in enumerate(((2, 0), (2, b_local // 2), (1, 0), (3, 0), (0, 0))):
        at = pl.multiple_of(lax.rem(pos[2] + step, 4) * b_local + skip, 8)
        copies.append(pltpu.make_async_copy(sums.at[pl.ds(at, outs[n].shape[0]), :], outs[n], sems.at[n]))
        copies[-1].start()
    for copy in copies:
        copy.wait()


def join_kernel(one, three, relay_up, relay_down, out_one, out_three):
    half = relay_up.shape[0]
    out_one[:half] = one[:half] + relay_up[...]
    out_one[half:] = one[half:]
    out_three[:half] = three[:half]
    out_three[half:] = three[half:] + relay_down[...]


def expand_kernel(pos, starts, first, target, g_ref, *refs):
    out_ref = refs[-1]
    b_local = refs[0].shape[0]
    x_local, oi, width = out_ref.shape[2], first.shape[0], 256
    sums = jnp.concatenate(two_terms(refs[0][...] + refs[1][...] + refs[2][...]), 0)
    b = pos[2] * b_local + lax.broadcasted_iota(I32, (b_local, 1), 0)
    wanted = label_of(b, starts) ^ target[pos[1]]

    def tile(n, _):
        x = n * width + lax.broadcasted_iota(I32, (1, width), 1)
        lanes = pl.ds(pl.multiple_of(n * width, width), width)
        a = pos[0] * (x_local // oi) + x // oi
        s = label_of(a, starts) ^ choose(x % oi, [first[i] for i in range(oi)])
        both = jnp.dot(sums, g_ref[:, lanes], preferred_element_type=F32)
        value = jnp.where(wanted == s, both[:b_local] + both[b_local:], 0.0)
        out_ref[0, :, lanes] = value + refs[3][0, :, lanes] if len(refs) > 4 else value
        return 0

    lax.fori_loop(0, x_local // width, tile, 0)


def params():
    return pltpu.CompilerParams(vmem_limit_bytes=48 * 1024 * 1024)


def one_pass(pos, starts, first, second, target, amplitudes, integrals, w_rows, before):
    k_local, c_local, x_local = amplitudes.shape
    v = c_local * 16
    b_local = v // 4
    shape = jax.ShapeDtypeStruct
    t0, hot = pl.pallas_call(
        pack_t_kernel,
        out_shape=(shape((k_local, c_local, LANES), F32), shape((LANES, x_local), BF16)),
        in_specs=[SMEM] * 4 + [VMEM],
        out_specs=(VMEM,) * 2,
        compiler_params=params(),
        name="pack_t",
    )(pos, starts, first, second, amplitudes)
    w0 = pl.pallas_call(
        pack_w_kernel,
        out_shape=shape((k_local, w_rows, BLOCK), F32),
        in_specs=[SMEM] * 4 + [VMEM],
        out_specs=VMEM,
        compiler_params=params(),
        cost_estimate=pl.CostEstimate(flops=10**9, bytes_accessed=4 * 10**6, transcendentals=0),
        name="pack_w",
    )(pos, starts, second, target, integrals)

    def along(x, axis, n, step):
        return lax.ppermute(x, axis, [(i, (i + step) % n) for i in range(n)])

    def swap(x):
        return lax.ppermute(x, "col", [(i, i ^ 1) for i in range(16)])

    got = [((0, 0), t0)]
    right = left = t0
    for n in range(1, 4):
        right = along(right, "col", 16, 2)
        left = along(left, "col", 16, -2)
        got += [((-n, 0), right), ((n, 0), left)]
    got += [((shift[0], 1), swap(piece)) for shift, piece in got]
    plan = [("t", shift) for shift, _ in got] + [("w", -n) for n in range(4)]
    pieces = [piece for _, piece in got] + [w0] + [along(w0, "row", 4, n) for n in range(1, 4)]
    late = [along(right[:1], "col", 16, 2), along(left[1:], "col", 16, -2)]
    total, w_late = pl.pallas_call(
        functools.partial(early_kernel, plan),
        out_shape=(shape((v + BLOCK, LANES), F32), shape((k_local, v // 8, BLOCK), F32)),
        in_specs=[SMEM] * 4 + [ANY] * len(pieces),
        out_specs=(VMEM,) * 2,
        scratch_shapes=[
            pltpu.VMEM((k_local, v, LANES), F32),
            pltpu.VMEM((k_local, v, BLOCK), F32),
            pltpu.SemaphoreType.DMA((len(pieces),)),
        ],
        compiler_params=params(),
        cost_estimate=pl.CostEstimate(flops=4 * 10**9, bytes_accessed=12 * 10**6, transcendentals=0),
        name="early",
    )(pos, starts, second, target, *pieces)
    late += [swap(piece) for piece in late]
    up, down, one, three, own = pl.pallas_call(
        late_kernel,
        out_shape=(shape((b_local // 2, LANES), F32),) * 2 + (shape((b_local, LANES), F32),) * 3,
        in_specs=[SMEM] * 4 + [ANY, VMEM] + [ANY] * 4,
        out_specs=(ANY,) * 5,
        scratch_shapes=[
            pltpu.VMEM((k_local, v // 8, LANES), F32),
            pltpu.VMEM((v + BLOCK, LANES), F32),
            pltpu.SemaphoreType.DMA((5,)),
        ],
        compiler_params=params(),
        name="late",
    )(pos, starts, second, target, total, w_late, *late)
    one, three = pl.pallas_call(
        join_kernel,
        out_shape=(shape((b_local, LANES), F32),) * 2,
        in_specs=[VMEM] * 4,
        out_specs=(VMEM,) * 2,
        compiler_params=params(),
        name="join",
    )(one, three, along(up, "depth", 4, 1), along(down, "depth", 4, -1))
    sums = [own, along(one, "depth", 4, 1), along(three, "depth", 4, -1)]
    more = [] if before is None else [before]
    return pl.pallas_call(
        expand_kernel,
        out_shape=shape((1, b_local, x_local), F32),
        in_specs=[SMEM] * 4 + [VMEM] * (4 + len(more)),
        out_specs=VMEM,
        compiler_params=params(),
        name="expand",
    )(pos, starts, first, target, hot, *sums, *more)


def per_device(amplitudes, integrals, irrep_virtual, irrep_first, irrep_second, irrep_target):
    v = irrep_virtual.shape[0]
    a_local = amplitudes.shape[2] // irrep_first.shape[0]
    starts = jnp.sum((irrep_virtual[None, :] < jnp.arange(16, dtype=I32)[:, None]).astype(I32), axis=1)
    where = [lax.axis_index(n).astype(I32) for n in ("row", "col", "depth")]

    def position(n_lane, n_block):
        return jnp.stack(where + [n_lane, n_block, 0, 0, 0]).astype(I32)

    w_rows = integrals.shape[1]
    flat = integrals.reshape(-1, 128)

    def run(n_lane, n_block, before):
        labels = (starts, irrep_first, irrep_second, irrep_target)
        return one_pass(position(n_lane, n_block), *labels, amplitudes, flat, w_rows, before)

    out = run(jnp.int32(0), jnp.int32(0), None)
    edges = jnp.arange(0, v, a_local, dtype=I32)
    low, high = starts[:8], starts[1:9]
    count = jnp.maximum(jnp.minimum(high, edges[:, None] + a_local) - jnp.maximum(low, edges[:, None]), 0)
    same = (jnp.arange(8)[:, None, None] ^ irrep_first[None, None, :]) == jnp.arange(8)[None, :, None]
    most = jnp.max(jnp.sum(count[:, None, :, None] * same[None].astype(I32), axis=(2, 3)))
    n_lanes = (most + LANES - 1) // LANES
    n_blocks = (jnp.max(high - low // 8 * 8) + BLOCK - 1) // BLOCK
    return lax.fori_loop(1, n_lanes * n_blocks, lambda n, acc: run(n % n_lanes, n // n_lanes, acc), out)


def solution(mesh):
    return jax.shard_map(
        per_device,
        mesh=mesh,
        in_specs=(P("depth", "col", "row"), P("depth", "row", "col", None), P(), P(), P(), P()),
        out_specs=P("col", "depth", "row"),
        check_vma=False,
    )
```

```python
import jax
import jax.numpy as jnp
from jax import lax
from jax.experimental import pallas as pl
from jax.experimental.pallas import tpu as pltpu
from jax.sharding import PartitionSpec as P


LANES = 512
BLOCK = 128
SMEM = pl.BlockSpec(memory_space=pltpu.SMEM)
VMEM = pl.BlockSpec(memory_space=pltpu.VMEM)
ANY = pl.BlockSpec(memory_space=pl.ANY)
F32, BF16, I32 = jnp.float32, jnp.bfloat16, jnp.int32


def label_of(place, starts):
    label = jnp.zeros_like(place)
    for irrep in range(1, 8):
        label = label + (place >= starts[irrep]).astype(I32)
    return label


def choose(index, scalars):
    out = jnp.full_like(index, scalars[0])
    for n in range(1, len(scalars)):
        out = jnp.where(index == n, scalars[n], out)
    return out


def two_terms(x):
    high = x.astype(BF16)
    return high, (x - high.astype(F32)).astype(BF16)


def nt(a, b):
    return lax.dot_general(a, b, (((1,), (1,)), ((), ())), preferred_element_type=F32)


def tn(a, b):
    return lax.dot_general(a, b, (((0,), (0,)), ((), ())), preferred_element_type=F32)


def x_places(pos, starts, first, x_local, oi):
    a_local = x_local // oi
    base = pos[0] * a_local
    x = lax.broadcasted_iota(I32, (1, x_local), 1)
    i = x % oi
    a = base + x // oi
    label = label_of(a, starts)
    firsts = [first[n] for n in range(oi)]
    s = label ^ choose(i, firsts)
    low = [jnp.maximum(starts[n], base) for n in range(8)]
    count = [jnp.maximum(jnp.minimum(starts[n + 1], base + a_local) - low[n], 0) for n in range(8)]
    place = a - choose(label, low)
    for n in range(oi - 1):
        place = place + jnp.where(n < i, choose(s ^ firsts[n], count), 0)
    return s, place - pos[3] * LANES


def pack_t_kernel(pos, starts, first, second, t_ref, out_ref, g_ref):
    k_local, c_local, x_local = t_ref.shape
    s, place = x_places(pos, starts, first, x_local, first.shape[0])
    c = pos[1] * c_local + lax.broadcasted_iota(I32, (c_local, 1), 0)
    label = label_of(c, starts)
    parts = []
    for k in range(k_local):
        keep = (label ^ second[pos[2] * k_local + k]) == s
        parts.extend(two_terms(jnp.where(keep, t_ref[k], 0.0)))
    stacked = jnp.concatenate(parts, 0)
    for n in range(LANES // 128):
        lanes = slice(n * 128, n * 128 + 128)
        rows = n * 128 + lax.broadcasted_iota(I32, (128, x_local), 0)
        hot = jnp.where(rows == place, 1.0, 0.0).astype(BF16)
        g_ref[lanes, :] = hot
        packed = nt(stacked, hot)
        for k in range(k_local):
            at = 2 * k * c_local
            out_ref[k, :, lanes] = packed[at : at + c_local] + packed[at + c_local : at + 2 * c_local]


def pack_w_kernel(pos, starts, second, target, w_ref, out_ref):
    k_local, c_local, _ = out_ref.shape
    rows = k_local * c_local
    tiles = w_ref.shape[0] // rows
    row = lax.broadcasted_iota(I32, (c_local, 1), 0)
    label = label_of(pos[0] * c_local + row, starts) ^ target[pos[1]]
    wanted = jnp.concatenate([label ^ second[pos[2] * k_local + k] for k in range(k_local)], 0)
    firsts = [starts[n] // 8 * 8 for n in range(8)]
    total = jnp.zeros((2 * rows, BLOCK), F32)
    for q in range(tiles):
        b = q * 128 + lax.broadcasted_iota(I32, (1, 128), 1)
        label_b = label_of(b, starts)
        place = b - choose(label_b, firsts) - pos[4] * BLOCK
        hot = jnp.where(lax.broadcasted_iota(I32, (BLOCK, 128), 0) == place, 1.0, 0.0).astype(BF16)
        w = jnp.where(wanted == label_b, w_ref[pl.ds(q, rows, stride=tiles), :], 0.0)
        total = total + nt(jnp.concatenate(two_terms(w), 0), hot)
    for k in range(k_local):
        out_ref[k] = total[k * c_local : (k + 1) * c_local] + total[rows + k * c_local : rows + (k + 1) * c_local]


def three_terms(w, t):
    w_high, w_low = two_terms(w)
    t_high, t_low = two_terms(t)
    both = tn(jnp.concatenate([w_high, w_low], 1), t_high)
    return both[: w.shape[1]] + both[w.shape[1] :] + tn(w_high, t_low)


def early_kernel(pos, starts, second, target, *refs):
    blocks, ws, (total, w_out, t_all, w_all, sems) = refs[:7], refs[7:11], refs[11:]
    k_local, c_all, _ = t_all.shape
    chip, core = pos[1] // 2, pos[1] % 2
    missing = c_all // 8
    half = missing // 2
    copies = []

    def fetch(piece, into, at):
        size = piece.shape[-2]
        there = into.at[:, pl.ds(pl.multiple_of(at, 8), size), :]
        copies.append(pltpu.make_async_copy(piece, there, sems.at[len(copies)]))
        copies[-1].start()

    for n, block in enumerate(blocks):
        far = n if n < 4 else 3 - n
        base = lax.rem(chip + (2 * core - 1) * far + 8, 8) * missing
        for window in range(2):
            of_core = core if (window == 0) == (n < 4) else 1 - core
            fetch(block.at[window], t_all, base + of_core * half)
    for n, w in enumerate(ws):
        fetch(w, w_all, lax.rem(pos[0] - n + 4, 4) * w.shape[1])
    at = pl.multiple_of(lax.rem(chip + 4, 8) * missing, 8)
    for k in range(k_local):
        t_all[k, pl.ds(at, missing), :] = jnp.zeros((missing, LANES), F32)
    total[...] = jnp.zeros_like(total)
    for copy in copies:
        copy.wait()
    w_out[...] = w_all[:, pl.ds(at, missing), :]
    row = lax.broadcasted_iota(I32, (128, 1), 0)

    def one_irrep(irrep, _):
        s = target[pos[1]] ^ irrep
        spans = []
        for k in range(k_local):
            p = s ^ second[pos[2] * k_local + k]
            spans.append((starts[p], starts[p + 1], starts[p] // 8 * 8))
        trips = [(end - aligned + 127) // 128 for _, end, aligned in spans]

        def step(n, acc):
            w_rows, t_rows = [], []
            for k, (begin, end, aligned) in enumerate(spans):
                nominal = aligned + n * 128
                at = pl.multiple_of(jnp.minimum(nominal, c_all - 128), 8)
                c = at + row
                keep = (c >= jnp.maximum(begin, nominal)) & (c < end)
                w_rows.append(jnp.where(keep, w_all[k, pl.ds(at, 128), :], 0.0))
                t_rows.append(t_all[k, pl.ds(at, 128), :])
            return acc + three_terms(jnp.concatenate(w_rows, 0), jnp.concatenate(t_rows, 0))

        sums = lax.fori_loop(0, jnp.maximum(*trips), step, jnp.zeros((BLOCK, LANES), F32))
        to = starts[irrep] // 8 * 8 + pos[4] * BLOCK

        @pl.when(to < starts[irrep + 1])
        def _():
            total[pl.ds(pl.multiple_of(to, 8), BLOCK), :] += sums

        return 0

    lax.fori_loop(0, 8, one_irrep, 0)


def rows_for(pos, total, step, part):
    b_local = (total.shape[0] - BLOCK) // 4
    at = lax.rem(pos[2] + step, 4) * b_local + part * (b_local // 2)
    return total[pl.ds(pl.multiple_of(at, 8), b_local // 2), :]


def late_kernel(pos, starts, second, target, given, w, mine, other, total, up, down, one, three, t_all):
    half = mine.shape[2]
    c_late = 2 * half
    chip, core = pos[1] // 2, pos[1] % 2
    for window in range(2):
        for piece, k in ((mine, core), (other, 1 - core)):
            of_core = core if (window == 0) == (piece is mine) else 1 - core
            t_all[k, pl.ds(pl.multiple_of(of_core * half, 8), half), :] = piece[window, 0]
    base = lax.rem(chip + 4, 8) * c_late
    label = label_of(base + lax.broadcasted_iota(I32, (c_late, 1), 0), starts)
    first_p = last_p = 0
    for irrep in range(1, 8):
        first_p = first_p + (base >= starts[irrep]).astype(I32)
        last_p = last_p + (base + c_late - 1 >= starts[irrep]).astype(I32)

    def one_p(p, _):
        for k in range(2):
            irrep = p ^ second[pos[2] * 2 + k] ^ target[pos[1]]
            term = three_terms(jnp.where(label == p, w[k], 0.0), t_all[k])
            to = starts[irrep] // 8 * 8 + pos[4] * BLOCK

            @pl.when(to < starts[irrep + 1])
            def _(term=term, to=to):
                total[pl.ds(pl.multiple_of(to, 8), BLOCK), :] += term

        return 0

    lax.fori_loop(first_p, last_p + 1, one_p, 0)
    for out, step, part in ((up, 2, 0), (down, 2, 1), (one, 1, 1), (three, 3, 0)):
        out[...] = rows_for(pos, total, step, part)


def join_kernel(pos, total, relay_up, relay_down, one, three):
    one[...] = rows_for(pos, total, 1, 0) + relay_up[...]
    three[...] = rows_for(pos, total, 3, 1) + relay_down[...]


def expand_kernel(pos, starts, first, target, g_ref, *refs):
    total, one_0, one_1, three_0, three_1 = refs[:5]
    out_ref = refs[-1]
    b_local = out_ref.shape[1]
    x_local, oi, width = out_ref.shape[2], first.shape[0], 256
    upper = rows_for(pos, total, 0, 0) + one_0[...] + three_0[...]
    lower = rows_for(pos, total, 0, 1) + one_1[...] + three_1[...]
    sums = jnp.concatenate(two_terms(jnp.concatenate([upper, lower], 0)), 0)
    b = pos[2] * b_local + lax.broadcasted_iota(I32, (b_local, 1), 0)
    wanted = label_of(b, starts) ^ target[pos[1]]

    def tile(n, _):
        x = n * width + lax.broadcasted_iota(I32, (1, width), 1)
        lanes = pl.ds(pl.multiple_of(n * width, width), width)
        a = pos[0] * (x_local // oi) + x // oi
        s = label_of(a, starts) ^ choose(x % oi, [first[i] for i in range(oi)])
        both = jnp.dot(sums, g_ref[:, lanes], preferred_element_type=F32)
        value = jnp.where(wanted == s, both[:b_local] + both[b_local:], 0.0)
        out_ref[0, :, lanes] = value + refs[5][0, :, lanes] if len(refs) > 6 else value
        return 0

    lax.fori_loop(0, x_local // width, tile, 0)


def params():
    return pltpu.CompilerParams(vmem_limit_bytes=48 * 1024 * 1024)


def one_pass(pos, starts, first, second, target, amplitudes, integrals, w_rows, before):
    k_local, c_local, x_local = amplitudes.shape
    v = c_local * 16
    b_local = v // 4
    shape = jax.ShapeDtypeStruct
    t0, hot = pl.pallas_call(
        pack_t_kernel,
        out_shape=(shape((k_local, c_local, LANES), F32), shape((LANES, x_local), BF16)),
        in_specs=[SMEM] * 4 + [VMEM],
        out_specs=(VMEM,) * 2,
        compiler_params=params(),
        name="pack_t",
    )(pos, starts, first, second, amplitudes)
    w0 = pl.pallas_call(
        pack_w_kernel,
        out_shape=shape((k_local, w_rows, BLOCK), F32),
        in_specs=[SMEM] * 4 + [VMEM],
        out_specs=VMEM,
        compiler_params=params(),
        cost_estimate=pl.CostEstimate(flops=10**9, bytes_accessed=4 * 10**6, transcendentals=0),
        name="pack_w",
    )(pos, starts, second, target, integrals)

    def along(x, axis, step):
        return lax.ppermute(x, axis, [(i, (i + step) % 4) for i in range(4)])

    def swap(x):
        return lax.ppermute(x, "col", [(i, i ^ 1) for i in range(16)])

    def ring(x):
        pairs = [(2 * z + core, 2 * ((z + 1 - 2 * core) % 8) + core) for z in range(8) for core in range(2)]
        return lax.ppermute(x, "col", pairs)

    got = [jnp.stack([t0, swap(t0)])]
    for _ in range(1, 4):
        got.append(ring(got[-1]))
    core = lax.axis_index("col") % 2
    mine = ring(lax.dynamic_slice_in_dim(got[3], core, 1, axis=1))
    got += [swap(got[n]) for n in range(1, 4)]
    ws = [w0] + [along(w0, "row", n) for n in range(1, 4)]
    total, w_late = pl.pallas_call(
        early_kernel,
        out_shape=(shape((v + BLOCK, LANES), F32), shape((k_local, v // 8, BLOCK), F32)),
        in_specs=[SMEM] * 4 + [ANY] * 11,
        out_specs=(VMEM,) * 2,
        scratch_shapes=[
            pltpu.VMEM((k_local, v, LANES), F32),
            pltpu.VMEM((k_local, v, BLOCK), F32),
            pltpu.SemaphoreType.DMA((18,)),
        ],
        compiler_params=params(),
        cost_estimate=pl.CostEstimate(flops=4 * 10**9, bytes_accessed=12 * 10**6, transcendentals=0),
        name="early",
    )(pos, starts, second, target, *got, *ws)
    part = shape((b_local // 2, LANES), F32)
    total, up, down, one_1, three_0 = pl.pallas_call(
        late_kernel,
        out_shape=(shape(total.shape, F32),) + (part,) * 4,
        in_specs=[SMEM] * 4 + [VMEM] * 4,
        out_specs=(VMEM,) * 5,
        scratch_shapes=[pltpu.VMEM((k_local, v // 8, LANES), F32)],
        input_output_aliases={4: 0},
        compiler_params=params(),
        name="late",
    )(pos, starts, second, target, total, w_late, mine, swap(mine))
    up, down = along(up, "depth", 1), along(down, "depth", -1)
    one_1, three_0 = along(one_1, "depth", 1), along(three_0, "depth", -1)
    one_0, three_1 = pl.pallas_call(
        join_kernel,
        out_shape=(part,) * 2,
        in_specs=[SMEM] + [VMEM] * 3,
        out_specs=(VMEM,) * 2,
        compiler_params=params(),
        name="join",
    )(pos, total, up, down)
    one_0, three_1 = along(one_0, "depth", 1), along(three_1, "depth", -1)
    sums = [total, one_0, one_1, three_0, three_1]
    more = [] if before is None else [before]
    return pl.pallas_call(
        expand_kernel,
        out_shape=shape((1, b_local, x_local), F32),
        in_specs=[SMEM] * 4 + [VMEM] * (6 + len(more)),
        out_specs=VMEM,
        compiler_params=params(),
        name="expand",
    )(pos, starts, first, target, hot, *sums, *more)


def per_device(amplitudes, integrals, irrep_virtual, irrep_first, irrep_second, irrep_target):
    v = irrep_virtual.shape[0]
    a_local = amplitudes.shape[2] // irrep_first.shape[0]
    starts = jnp.sum((irrep_virtual[None, :] < jnp.arange(16, dtype=I32)[:, None]).astype(I32), axis=1)
    where = [lax.axis_index(n).astype(I32) for n in ("row", "col", "depth")]

    def position(n_lane, n_block):
        return jnp.stack(where + [n_lane, n_block, 0, 0, 0]).astype(I32)

    w_rows = integrals.shape[1]
    flat = integrals.reshape(-1, 128)

    def run(n_lane, n_block, before):
        labels = (starts, irrep_first, irrep_second, irrep_target)
        return one_pass(position(n_lane, n_block), *labels, amplitudes, flat, w_rows, before)

    out = run(jnp.int32(0), jnp.int32(0), None)
    edges = jnp.arange(0, v, a_local, dtype=I32)
    low, high = starts[:8], starts[1:9]
    count = jnp.maximum(jnp.minimum(high, edges[:, None] + a_local) - jnp.maximum(low, edges[:, None]), 0)
    same = (jnp.arange(8)[:, None, None] ^ irrep_first[None, None, :]) == jnp.arange(8)[None, :, None]
    most = jnp.max(jnp.sum(count[:, None, :, None] * same[None].astype(I32), axis=(2, 3)))
    n_lanes = (most + LANES - 1) // LANES
    n_blocks = (jnp.max(high - low // 8 * 8) + BLOCK - 1) // BLOCK
    return lax.fori_loop(1, n_lanes * n_blocks, lambda n, acc: run(n % n_lanes, n // n_lanes, acc), out)


def solution(mesh):
    return jax.shard_map(
        per_device,
        mesh=mesh,
        in_specs=(P("depth", "col", "row"), P("depth", "row", "col", None), P(), P(), P(), P()),
        out_specs=P("col", "depth", "row"),
        check_vma=False,
    )
```

```python
import functools

import jax
import jax.numpy as jnp
from jax import lax
from jax.experimental import pallas as pl
from jax.experimental.pallas import tpu as pltpu
from jax.sharding import PartitionSpec as P


LANES = 512
BLOCK = 128
SMEM = pl.BlockSpec(memory_space=pltpu.SMEM)
VMEM = pl.BlockSpec(memory_space=pltpu.VMEM)
ANY = pl.BlockSpec(memory_space=pl.ANY)
F32, BF16, I32 = jnp.float32, jnp.bfloat16, jnp.int32


def label_of(place, starts):
    label = jnp.zeros_like(place)
    for irrep in range(1, 8):
        label = label + (place >= starts[irrep]).astype(I32)
    return label


def choose(index, scalars):
    out = jnp.full_like(index, scalars[0])
    for n in range(1, len(scalars)):
        out = jnp.where(index == n, scalars[n], out)
    return out


def two_terms(x):
    high = x.astype(BF16)
    return high, (x - high.astype(F32)).astype(BF16)


def nt(a, b):
    return lax.dot_general(a, b, (((1,), (1,)), ((), ())), preferred_element_type=F32)


def tn(a, b):
    return lax.dot_general(a, b, (((0,), (0,)), ((), ())), preferred_element_type=F32)


def x_places(pos, starts, first, x_local, oi):
    a_local = x_local // oi
    base = pos[0] * a_local
    x = lax.broadcasted_iota(I32, (1, x_local), 1)
    i = x % oi
    a = base + x // oi
    label = label_of(a, starts)
    firsts = [first[n] for n in range(oi)]
    s = label ^ choose(i, firsts)
    low = [jnp.maximum(starts[n], base) for n in range(8)]
    count = [jnp.maximum(jnp.minimum(starts[n + 1], base + a_local) - low[n], 0) for n in range(8)]
    place = a - choose(label, low)
    for n in range(oi - 1):
        place = place + jnp.where(n < i, choose(s ^ firsts[n], count), 0)
    return s, place - pos[3] * LANES


def pack_t_kernel(pos, starts, first, second, t_ref, out_ref, g_ref):
    k_local, c_local, x_local = t_ref.shape
    s, place = x_places(pos, starts, first, x_local, first.shape[0])
    c = pos[1] * c_local + lax.broadcasted_iota(I32, (c_local, 1), 0)
    label = label_of(c, starts)
    parts = []
    for k in range(k_local):
        keep = (label ^ second[pos[2] * k_local + k]) == s
        parts.extend(two_terms(jnp.where(keep, t_ref[k], 0.0)))
    stacked = jnp.concatenate(parts, 0)
    for n in range(LANES // 128):
        lanes = slice(n * 128, n * 128 + 128)
        rows = n * 128 + lax.broadcasted_iota(I32, (128, x_local), 0)
        hot = jnp.where(rows == place, 1.0, 0.0).astype(BF16)
        g_ref[lanes, :] = hot
        packed = nt(stacked, hot)
        for k in range(k_local):
            at = 2 * k * c_local
            out_ref[k, :, lanes] = packed[at : at + c_local] + packed[at + c_local : at + 2 * c_local]


def pack_w_kernel(pos, starts, second, target, w_ref, out_ref):
    k_local, c_local, _ = out_ref.shape
    rows = k_local * c_local
    tiles = w_ref.shape[0] // rows
    row = lax.broadcasted_iota(I32, (c_local, 1), 0)
    label = label_of(pos[0] * c_local + row, starts) ^ target[pos[1]]
    wanted = jnp.concatenate([label ^ second[pos[2] * k_local + k] for k in range(k_local)], 0)
    firsts = [starts[n] // 8 * 8 for n in range(8)]
    total = jnp.zeros((2 * rows, BLOCK), F32)
    for q in range(tiles):
        b = q * 128 + lax.broadcasted_iota(I32, (1, 128), 1)
        label_b = label_of(b, starts)
        place = b - choose(label_b, firsts) - pos[4] * BLOCK
        hot = jnp.where(lax.broadcasted_iota(I32, (BLOCK, 128), 0) == place, 1.0, 0.0).astype(BF16)
        w = jnp.where(wanted == label_b, w_ref[pl.ds(q, rows, stride=tiles), :], 0.0)
        total = total + nt(jnp.concatenate(two_terms(w), 0), hot)
    for k in range(k_local):
        out_ref[k] = total[k * c_local : (k + 1) * c_local] + total[rows + k * c_local : rows + (k + 1) * c_local]


def three_terms(w, t):
    w_high, w_low = two_terms(w)
    t_high, t_low = two_terms(t)
    both = tn(jnp.concatenate([w_high, w_low], 1), t_high)
    return both[: w.shape[1]] + both[w.shape[1] :] + tn(w_high, t_low)


def fetch_windows(pos, windows, into, sems):
    copies = []
    for n, ((far, other), piece) in enumerate(windows):
        core = 1 - pos[1] % 2 if other else pos[1] % 2
        at = (lax.rem(pos[1] // 2 + far + 8, 8) * 2 + core) * piece.shape[1]
        there = into.at[:, pl.ds(pl.multiple_of(at, 8), piece.shape[1]), :]
        copies.append(pltpu.make_async_copy(piece, there, sems.at[n]))
        copies[-1].start()
    return copies


def place_kernel(where, pos, *refs):
    pieces, (t_all, sems) = refs[: len(where)], refs[len(where) :]
    for copy in fetch_windows(pos, list(zip(where, pieces)), t_all, sems):
        copy.wait()


def early_kernel(where, pos, starts, second, target, given, *refs):
    pieces, ws, (t_all, total, w_out, w_all, sems) = refs[: len(where)], refs[len(where) : len(where) + 4], refs[len(where) + 4 :]
    k_local, c_all, _ = t_all.shape
    chip = pos[1] // 2
    missing = c_all // 8
    copies = fetch_windows(pos, list(zip(where, pieces)), t_all, sems)
    for n, w in enumerate(ws):
        at = pl.multiple_of(lax.rem(pos[0] - n + 4, 4) * w.shape[1], 8)
        copies.append(pltpu.make_async_copy(w, w_all.at[:, pl.ds(at, w.shape[1]), :], sems.at[len(where) + n]))
        copies[-1].start()
    at = pl.multiple_of(lax.rem(chip + 4, 8) * missing, 8)
    for k in range(k_local):
        t_all[k, pl.ds(at, missing), :] = jnp.zeros((missing, LANES), F32)
    total[...] = jnp.zeros_like(total)
    for copy in copies:
        copy.wait()
    w_out[...] = w_all[:, pl.ds(at, missing), :]
    row = lax.broadcasted_iota(I32, (128, 1), 0)

    def one_irrep(irrep, _):
        s = target[pos[1]] ^ irrep
        spans = []
        for k in range(k_local):
            p = s ^ second[pos[2] * k_local + k]
            spans.append((starts[p], starts[p + 1], starts[p] // 8 * 8))
        trips = [(end - aligned + 127) // 128 for _, end, aligned in spans]

        def step(n, acc):
            w_rows, t_rows = [], []
            for k, (begin, end, aligned) in enumerate(spans):
                nominal = aligned + n * 128
                at = pl.multiple_of(jnp.minimum(nominal, c_all - 128), 8)
                c = at + row
                keep = (c >= jnp.maximum(begin, nominal)) & (c < end)
                w_rows.append(jnp.where(keep, w_all[k, pl.ds(at, 128), :], 0.0))
                t_rows.append(t_all[k, pl.ds(at, 128), :])
            return acc + three_terms(jnp.concatenate(w_rows, 0), jnp.concatenate(t_rows, 0))

        sums = lax.fori_loop(0, jnp.maximum(*trips), step, jnp.zeros((BLOCK, LANES), F32))
        to = starts[irrep] // 8 * 8 + pos[4] * BLOCK

        @pl.when(to < starts[irrep + 1])
        def _():
            total[pl.ds(pl.multiple_of(to, 8), BLOCK), :] += sums

        return 0

    lax.fori_loop(0, 8, one_irrep, 0)


def rows_for(pos, total, step, part):
    b_local = (total.shape[0] - BLOCK) // 4
    at = lax.rem(pos[2] + step, 4) * b_local + part * (b_local // 2)
    return total[pl.ds(pl.multiple_of(at, 8), b_local // 2), :]


def late_kernel(pos, starts, second, target, given, w, t0, t1, u0, u1, total, up, down, one, three, t_all):
    half = t0.shape[1]
    c_late = 2 * half
    chip, core = pos[1] // 2, pos[1] % 2
    for k, of_core, piece in ((0, core, t0), (1, core, t1), (0, 1 - core, u0), (1, 1 - core, u1)):
        t_all[k, pl.ds(pl.multiple_of(of_core * half, 8), half), :] = piece[0]
    base = lax.rem(chip + 4, 8) * c_late
    label = label_of(base + lax.broadcasted_iota(I32, (c_late, 1), 0), starts)
    first_p = last_p = 0
    for irrep in range(1, 8):
        first_p = first_p + (base >= starts[irrep]).astype(I32)
        last_p = last_p + (base + c_late - 1 >= starts[irrep]).astype(I32)

    def one_p(p, _):
        for k in range(2):
            irrep = p ^ second[pos[2] * 2 + k] ^ target[pos[1]]
            term = three_terms(jnp.where(label == p, w[k], 0.0), t_all[k])
            to = starts[irrep] // 8 * 8 + pos[4] * BLOCK

            @pl.when(to < starts[irrep + 1])
            def _(term=term, to=to):
                total[pl.ds(pl.multiple_of(to, 8), BLOCK), :] += term

        return 0

    lax.fori_loop(first_p, last_p + 1, one_p, 0)
    for out, step, part in ((up, 2, 0), (down, 2, 1), (one, 1, 1), (three, 3, 0)):
        out[...] = rows_for(pos, total, step, part)


def join_kernel(pos, total, relay_up, relay_down, one, three):
    one[...] = rows_for(pos, total, 1, 0) + relay_up[...]
    three[...] = rows_for(pos, total, 3, 1) + relay_down[...]


def expand_kernel(pos, starts, first, target, g_ref, *refs):
    total, one_0, one_1, three_0, three_1 = refs[:5]
    out_ref = refs[-1]
    b_local = out_ref.shape[1]
    x_local, oi, width = out_ref.shape[2], first.shape[0], 256
    upper = rows_for(pos, total, 0, 0) + one_0[...] + three_0[...]
    lower = rows_for(pos, total, 0, 1) + one_1[...] + three_1[...]
    sums = jnp.concatenate(two_terms(jnp.concatenate([upper, lower], 0)), 0)
    b = pos[2] * b_local + lax.broadcasted_iota(I32, (b_local, 1), 0)
    wanted = label_of(b, starts) ^ target[pos[1]]

    def tile(n, _):
        x = n * width + lax.broadcasted_iota(I32, (1, width), 1)
        lanes = pl.ds(pl.multiple_of(n * width, width), width)
        a = pos[0] * (x_local // oi) + x // oi
        s = label_of(a, starts) ^ choose(x % oi, [first[i] for i in range(oi)])
        both = jnp.dot(sums, g_ref[:, lanes], preferred_element_type=F32)
        value = jnp.where(wanted == s, both[:b_local] + both[b_local:], 0.0)
        out_ref[0, :, lanes] = value + refs[5][0, :, lanes] if len(refs) > 6 else value
        return 0

    lax.fori_loop(0, x_local // width, tile, 0)


def params():
    return pltpu.CompilerParams(vmem_limit_bytes=24 * 1024 * 1024)


def one_pass(pos, starts, first, second, target, amplitudes, integrals, w_rows, before):
    k_local, c_local, x_local = amplitudes.shape
    v = c_local * 16
    b_local = v // 4
    shape = jax.ShapeDtypeStruct
    t0, hot = pl.pallas_call(
        pack_t_kernel,
        out_shape=(shape((k_local, c_local, LANES), F32), shape((LANES, x_local), BF16)),
        in_specs=[SMEM] * 4 + [VMEM],
        out_specs=(VMEM,) * 2,
        compiler_params=params(),
        name="pack_t",
    )(pos, starts, first, second, amplitudes)
    w0 = pl.pallas_call(
        pack_w_kernel,
        out_shape=shape((k_local, w_rows, BLOCK), F32),
        in_specs=[SMEM] * 4 + [VMEM],
        out_specs=VMEM,
        compiler_params=params(),
        cost_estimate=pl.CostEstimate(flops=10**9, bytes_accessed=4 * 10**6, transcendentals=0),
        name="pack_w",
    )(pos, starts, second, target, integrals)

    def along(x, axis, step):
        return lax.ppermute(x, axis, [(i, (i + step) % 4) for i in range(4)])

    def swap(x):
        return lax.ppermute(x, "col", [(i, i ^ 1) for i in range(16)])

    def ring(x, step):
        return lax.ppermute(x, "col", [(i, (i + 2 * step) % 16) for i in range(16)])

    got = {(0, False): t0}
    right = left = t0
    for n in range(1, 4):
        right, left = ring(right, 1), ring(left, -1)
        got[-n, False], got[n, False] = right, left
    late = [ring(right[:1], 1), ring(left[1:], -1)]
    for (far, _), piece in list(got.items()):
        got[far, True] = swap(piece)
    ws = [w0] + [along(w0, "row", n) for n in range(1, 4)]
    arrived = [place for place in got if abs(place[0]) <= (1 if place[1] else 2)]
    others = [place for place in got if place not in arrived]
    t_all = pl.pallas_call(
        functools.partial(place_kernel, arrived),
        out_shape=shape((k_local, v, LANES), F32),
        in_specs=[SMEM] + [ANY] * len(arrived),
        out_specs=VMEM,
        scratch_shapes=[pltpu.SemaphoreType.DMA((len(arrived),))],
        compiler_params=params(),
        cost_estimate=pl.CostEstimate(flops=0, bytes_accessed=3 * 10**6, transcendentals=0),
        name="place",
    )(pos, *[got[place] for place in arrived])
    _, total, w_late = pl.pallas_call(
        functools.partial(early_kernel, others),
        out_shape=(
            shape(t_all.shape, F32),
            shape((v + BLOCK, LANES), F32),
            shape((k_local, v // 8, BLOCK), F32),
        ),
        in_specs=[SMEM] * 4 + [VMEM] + [ANY] * (len(others) + 4),
        out_specs=(VMEM,) * 3,
        scratch_shapes=[pltpu.VMEM((k_local, v, BLOCK), F32), pltpu.SemaphoreType.DMA((len(others) + 4,))],
        input_output_aliases={4: 0},
        compiler_params=params(),
        cost_estimate=pl.CostEstimate(flops=4 * 10**9, bytes_accessed=12 * 10**6, transcendentals=0),
        name="early",
    )(pos, starts, second, target, t_all, *[got[place] for place in others], *ws)
    late += [swap(piece) for piece in late]
    part = shape((b_local // 2, LANES), F32)
    total, up, down, one_1, three_0 = pl.pallas_call(
        late_kernel,
        out_shape=(shape(total.shape, F32),) + (part,) * 4,
        in_specs=[SMEM] * 4 + [VMEM] * 6,
        out_specs=(VMEM,) * 5,
        scratch_shapes=[pltpu.VMEM((k_local, v // 8, LANES), F32)],
        input_output_aliases={4: 0},
        compiler_params=params(),
        name="late",
    )(pos, starts, second, target, total, w_late, *late)
    up, down = along(up, "depth", 1), along(down, "depth", -1)
    one_1, three_0 = along(one_1, "depth", 1), along(three_0, "depth", -1)
    one_0, three_1 = pl.pallas_call(
        join_kernel,
        out_shape=(part,) * 2,
        in_specs=[SMEM] + [VMEM] * 3,
        out_specs=(VMEM,) * 2,
        compiler_params=params(),
        name="join",
    )(pos, total, up, down)
    one_0, three_1 = along(one_0, "depth", 1), along(three_1, "depth", -1)
    sums = [total, one_0, one_1, three_0, three_1]
    more = [] if before is None else [before]
    return pl.pallas_call(
        expand_kernel,
        out_shape=shape((1, b_local, x_local), F32),
        in_specs=[SMEM] * 4 + [VMEM] * (6 + len(more)),
        out_specs=VMEM,
        compiler_params=params(),
        name="expand",
    )(pos, starts, first, target, hot, *sums, *more)


def per_device(amplitudes, integrals, irrep_virtual, irrep_first, irrep_second, irrep_target):
    v = irrep_virtual.shape[0]
    a_local = amplitudes.shape[2] // irrep_first.shape[0]
    starts = jnp.sum((irrep_virtual[None, :] < jnp.arange(16, dtype=I32)[:, None]).astype(I32), axis=1)
    where = [lax.axis_index(n).astype(I32) for n in ("row", "col", "depth")]

    def position(n_lane, n_block):
        return jnp.stack(where + [n_lane, n_block, 0, 0, 0]).astype(I32)

    w_rows = integrals.shape[1]
    flat = integrals.reshape(-1, 128)

    def run(n_lane, n_block, before):
        labels = (starts, irrep_first, irrep_second, irrep_target)
        return one_pass(position(n_lane, n_block), *labels, amplitudes, flat, w_rows, before)

    out = run(jnp.int32(0), jnp.int32(0), None)
    edges = jnp.arange(0, v, a_local, dtype=I32)
    low, high = starts[:8], starts[1:9]
    count = jnp.maximum(jnp.minimum(high, edges[:, None] + a_local) - jnp.maximum(low, edges[:, None]), 0)
    same = (jnp.arange(8)[:, None, None] ^ irrep_first[None, None, :]) == jnp.arange(8)[None, :, None]
    most = jnp.max(jnp.sum(count[:, None, :, None] * same[None].astype(I32), axis=(2, 3)))
    n_lanes = (most + LANES - 1) // LANES
    n_blocks = (jnp.max(high - low // 8 * 8) + BLOCK - 1) // BLOCK
    return lax.fori_loop(1, n_lanes * n_blocks, lambda n, acc: run(n % n_lanes, n // n_lanes, acc), out)


def solution(mesh):
    return jax.shard_map(
        per_device,
        mesh=mesh,
        in_specs=(P("depth", "col", "row"), P("depth", "row", "col", None), P(), P(), P(), P()),
        out_specs=P("col", "depth", "row"),
        check_vma=False,
    )
```

```python
import functools

import jax
import jax.numpy as jnp
from jax import lax
from jax.experimental import pallas as pl
from jax.experimental.pallas import tpu as pltpu
from jax.sharding import PartitionSpec as P


LANES = 512
BLOCK = 128
SMEM = pl.BlockSpec(memory_space=pltpu.SMEM)
VMEM = pl.BlockSpec(memory_space=pltpu.VMEM)
ANY = pl.BlockSpec(memory_space=pl.ANY)
F32, BF16, I32 = jnp.float32, jnp.bfloat16, jnp.int32


def label_of(place, starts):
    label = jnp.zeros_like(place)
    for irrep in range(1, 8):
        label = label + (place >= starts[irrep]).astype(I32)
    return label


def choose(index, scalars):
    out = jnp.full_like(index, scalars[0])
    for n in range(1, len(scalars)):
        out = jnp.where(index == n, scalars[n], out)
    return out


def two_terms(x):
    high = x.astype(BF16)
    return high, (x - high.astype(F32)).astype(BF16)


def nt(a, b):
    return lax.dot_general(a, b, (((1,), (1,)), ((), ())), preferred_element_type=F32)


def tn(a, b):
    return lax.dot_general(a, b, (((0,), (0,)), ((), ())), preferred_element_type=F32)


def x_places(pos, starts, first, x_local, oi):
    a_local = x_local // oi
    base = pos[0] * a_local
    x = lax.broadcasted_iota(I32, (1, x_local), 1)
    i = x % oi
    a = base + x // oi
    label = label_of(a, starts)
    firsts = [first[n] for n in range(oi)]
    s = label ^ choose(i, firsts)
    low = [jnp.maximum(starts[n], base) for n in range(8)]
    count = [jnp.maximum(jnp.minimum(starts[n + 1], base + a_local) - low[n], 0) for n in range(8)]
    place = a - choose(label, low)
    for n in range(oi - 1):
        place = place + jnp.where(n < i, choose(s ^ firsts[n], count), 0)
    return s, place - pos[3] * LANES


def pack_t_kernel(pos, starts, first, second, t_ref, out_ref, g_ref):
    k_local, c_local, x_local = t_ref.shape
    s, place = x_places(pos, starts, first, x_local, first.shape[0])
    c = pos[1] * c_local + lax.broadcasted_iota(I32, (c_local, 1), 0)
    label = label_of(c, starts)
    parts = []
    for k in range(k_local):
        keep = (label ^ second[pos[2] * k_local + k]) == s
        parts.extend(two_terms(jnp.where(keep, t_ref[k], 0.0)))
    stacked = jnp.concatenate(parts, 0)
    for n in range(LANES // 128):
        lanes = slice(n * 128, n * 128 + 128)
        rows = n * 128 + lax.broadcasted_iota(I32, (128, x_local), 0)
        hot = jnp.where(rows == place, 1.0, 0.0).astype(BF16)
        g_ref[lanes, :] = hot
        packed = nt(stacked, hot)
        for k in range(k_local):
            at = 2 * k * c_local
            out_ref[k, :, lanes] = packed[at : at + c_local] + packed[at + c_local : at + 2 * c_local]


def pack_w_kernel(pos, starts, second, target, w_ref, out_ref):
    k_local, c_local, _ = out_ref.shape
    rows = k_local * c_local
    tiles = w_ref.shape[0] // rows
    row = lax.broadcasted_iota(I32, (c_local, 1), 0)
    label = label_of(pos[0] * c_local + row, starts) ^ target[pos[1]]
    wanted = jnp.concatenate([label ^ second[pos[2] * k_local + k] for k in range(k_local)], 0)
    firsts = [starts[n] // 8 * 8 for n in range(8)]
    total = jnp.zeros((2 * rows, BLOCK), F32)
    for q in range(tiles):
        b = q * 128 + lax.broadcasted_iota(I32, (1, 128), 1)
        label_b = label_of(b, starts)
        place = b - choose(label_b, firsts) - pos[4] * BLOCK
        hot = jnp.where(lax.broadcasted_iota(I32, (BLOCK, 128), 0) == place, 1.0, 0.0).astype(BF16)
        w = jnp.where(wanted == label_b, w_ref[pl.ds(q, rows, stride=tiles), :], 0.0)
        total = total + nt(jnp.concatenate(two_terms(w), 0), hot)
    for k in range(k_local):
        out_ref[k] = total[k * c_local : (k + 1) * c_local] + total[rows + k * c_local : rows + (k + 1) * c_local]


def three_terms(w, t):
    w_high, w_low = two_terms(w)
    t_high, t_low = two_terms(t)
    both = tn(jnp.concatenate([w_high, w_low], 1), t_high)
    return both[: w.shape[1]] + both[w.shape[1] :] + tn(w_high, t_low)


def put_window(pos, place, piece, into, k=None):
    size = piece.shape[1]
    core = 1 - pos[1] % 2 if place[1] else pos[1] % 2
    at = (lax.rem(pos[1] // 2 + place[0] + 8, 8) * 2 + core) * size
    rows = pl.ds(pl.multiple_of(at, 8), size)
    for n in range(piece.shape[0]):
        into[n if k is None else k, rows, :] = piece[n]


def place_kernel(where, pos, *refs):
    pieces, (own, pair, far), (t_all, w_all) = refs[: len(where)], refs[len(where) : -2], refs[-2:]
    for place, piece in zip(where, pieces):
        put_window(pos, place, piece, t_all)
    size = own.shape[1]
    r = pos[0]
    for row, piece in ((r, own), (r ^ 1, pair), (3 - r, far.at[0]), ((3 - r) ^ 1, far.at[1])):
        for k in range(own.shape[0]):
            w_all[k, pl.ds(pl.multiple_of(row * size, 8), size), :] = piece[k]


def rows_for(pos, total, step, part):
    b_local = (total.shape[0] - BLOCK) // 4
    at = lax.rem(pos[2] + step, 4) * b_local + part * (b_local // 2)
    return total[pl.ds(pl.multiple_of(at, 8), b_local // 2), :]


def product_kernel(where, pos, starts, second, target, given, w_all, *refs):
    pieces, (t_all, total, up, down, one, three) = refs[: len(where)], refs[len(where) :]
    k_local, c_all, _ = t_all.shape
    for (k, place), piece in zip(where, pieces):
        put_window(pos, place, piece, t_all, k)
    total[...] = jnp.zeros_like(total)
    row = lax.broadcasted_iota(I32, (128, 1), 0)

    def one_irrep(irrep, _):
        s = target[pos[1]] ^ irrep
        to = starts[irrep] // 8 * 8 + pos[4] * BLOCK
        spans = []
        for k in range(k_local):
            p = s ^ second[pos[2] * k_local + k]
            spans.append((starts[p], starts[p + 1], starts[p] // 8 * 8))
        trips = jnp.maximum(*[(end - aligned + 127) // 128 for _, end, aligned in spans])

        def step(n, _):
            w_rows, t_rows = [], []
            for k, (begin, end, aligned) in enumerate(spans):
                nominal = aligned + n * 128
                at = pl.multiple_of(jnp.minimum(nominal, c_all - 128), 8)
                c = at + row
                keep = (c >= jnp.maximum(begin, nominal)) & (c < end)
                w_rows.append(jnp.where(keep, w_all[k, pl.ds(at, 128), :], 0.0))
                t_rows.append(t_all[k, pl.ds(at, 128), :])
            term = three_terms(jnp.concatenate(w_rows, 0), jnp.concatenate(t_rows, 0))
            total[pl.ds(pl.multiple_of(to, 8), BLOCK), :] += term
            return 0

        return lax.fori_loop(0, jnp.where(to < starts[irrep + 1], trips, 0), step, 0)

    lax.fori_loop(0, 8, one_irrep, 0)
    for out, step, part in ((up, 2, 0), (down, 2, 1), (one, 1, 1), (three, 3, 0)):
        out[...] = rows_for(pos, total, step, part)


def join_kernel(pos, total, relay_up, relay_down, one, three):
    one[...] = rows_for(pos, total, 1, 0) + relay_up[...]
    three[...] = rows_for(pos, total, 3, 1) + relay_down[...]


def expand_kernel(pos, starts, first, target, g_ref, *refs):
    total, one_0, one_1, three_0, three_1 = refs[:5]
    out_ref = refs[-1]
    b_local = out_ref.shape[1]
    x_local, oi, width = out_ref.shape[2], first.shape[0], 256
    upper = rows_for(pos, total, 0, 0) + one_0[...] + three_0[...]
    lower = rows_for(pos, total, 0, 1) + one_1[...] + three_1[...]
    sums = jnp.concatenate(two_terms(jnp.concatenate([upper, lower], 0)), 0)
    b = pos[2] * b_local + lax.broadcasted_iota(I32, (b_local, 1), 0)
    wanted = label_of(b, starts) ^ target[pos[1]]

    def tile(n, _):
        x = n * width + lax.broadcasted_iota(I32, (1, width), 1)
        lanes = pl.ds(pl.multiple_of(n * width, width), width)
        a = pos[0] * (x_local // oi) + x // oi
        s = label_of(a, starts) ^ choose(x % oi, [first[i] for i in range(oi)])
        both = jnp.dot(sums, g_ref[:, lanes], preferred_element_type=F32)
        value = jnp.where(wanted == s, both[:b_local] + both[b_local:], 0.0)
        out_ref[0, :, lanes] = value + refs[5][0, :, lanes] if len(refs) > 6 else value
        return 0

    lax.fori_loop(0, x_local // width, tile, 0)


def params(mib=16):
    return pltpu.CompilerParams(vmem_limit_bytes=mib * 1024 * 1024)


def one_pass(pos, starts, first, second, target, amplitudes, integrals, w_rows, before):
    k_local, c_local, x_local = amplitudes.shape
    v = c_local * 16
    b_local = v // 4
    shape = jax.ShapeDtypeStruct
    t0, hot = pl.pallas_call(
        pack_t_kernel,
        out_shape=(shape((k_local, c_local, LANES), F32), shape((LANES, x_local), BF16)),
        in_specs=[SMEM] * 4 + [VMEM],
        out_specs=(VMEM,) * 2,
        compiler_params=params(),
        name="pack_t",
    )(pos, starts, first, second, amplitudes)
    w0 = pl.pallas_call(
        pack_w_kernel,
        out_shape=shape((k_local, w_rows, BLOCK), F32),
        in_specs=[SMEM] * 4 + [VMEM],
        out_specs=VMEM,
        compiler_params=params(),
        cost_estimate=pl.CostEstimate(flops=10**9, bytes_accessed=4 * 10**6, transcendentals=0),
        name="pack_w",
    )(pos, starts, second, target, integrals)

    def along(x, axis, step):
        return lax.ppermute(x, axis, [(i, (i + step) % 4) for i in range(4)])

    def swap(x):
        return lax.ppermute(x, "col", [(i, i ^ 1) for i in range(16)])

    def ring(x, step):
        return lax.ppermute(x, "col", [(i, (i + 2 * step) % 16) for i in range(16)])

    got = {(0, False): t0}
    right = left = t0
    for n in range(1, 4):
        right, left = ring(right, 1), ring(left, -1)
        got[-n, False], got[n, False] = right, left
    late = [ring(right[:1], 1), ring(left[1:], -1)]
    for (far, _), piece in list(got.items()):
        got[far, True] = swap(piece)
    pair = lax.ppermute(w0, "row", [(i, i ^ 1) for i in range(4)])
    far = lax.ppermute(jnp.stack([w0, pair]), "row", [(i, 3 - i) for i in range(4)])
    t_all, w_all = pl.pallas_call(
        functools.partial(place_kernel, list(got)),
        out_shape=(shape((k_local, v, LANES), F32), shape((k_local, v, BLOCK), F32)),
        in_specs=[SMEM] + [VMEM] * (len(got) + 3),
        out_specs=(VMEM,) * 2,
        compiler_params=params(),
        cost_estimate=pl.CostEstimate(flops=0, bytes_accessed=7 * 10**6, transcendentals=0),
        name="place",
    )(pos, *got.values(), w0, pair, far)
    late += [swap(piece) for piece in late]
    where = [(0, (4, False)), (1, (4, False)), (0, (4, True)), (1, (4, True))]
    part = shape((b_local // 2, LANES), F32)
    _, total, up, down, one_1, three_0 = pl.pallas_call(
        functools.partial(product_kernel, where),
        out_shape=(shape(t_all.shape, F32), shape((v + BLOCK, LANES), F32)) + (part,) * 4,
        in_specs=[SMEM] * 4 + [VMEM] * 6,
        out_specs=(VMEM,) * 6,
        input_output_aliases={4: 0},
        compiler_params=params(),
        name="product",
    )(pos, starts, second, target, t_all, w_all, *late)
    up, down = along(up, "depth", 1), along(down, "depth", -1)
    one_1, three_0 = along(one_1, "depth", 1), along(three_0, "depth", -1)
    one_0, three_1 = pl.pallas_call(
        join_kernel,
        out_shape=(part,) * 2,
        in_specs=[SMEM] + [VMEM] * 3,
        out_specs=(VMEM,) * 2,
        compiler_params=params(4),
        name="join",
    )(pos, total, up, down)
    one_0, three_1 = along(one_0, "depth", 1), along(three_1, "depth", -1)
    sums = [total, one_0, one_1, three_0, three_1]
    more = [] if before is None else [before]
    return pl.pallas_call(
        expand_kernel,
        out_shape=shape((1, b_local, x_local), F32),
        in_specs=[SMEM] * 4 + [VMEM] * (6 + len(more)),
        out_specs=VMEM,
        compiler_params=params(),
        name="expand",
    )(pos, starts, first, target, hot, *sums, *more)


def per_device(amplitudes, integrals, irrep_virtual, irrep_first, irrep_second, irrep_target):
    v = irrep_virtual.shape[0]
    a_local = amplitudes.shape[2] // irrep_first.shape[0]
    starts = jnp.sum((irrep_virtual[None, :] < jnp.arange(16, dtype=I32)[:, None]).astype(I32), axis=1)
    where = [lax.axis_index(n).astype(I32) for n in ("row", "col", "depth")]

    def position(n_lane, n_block):
        return jnp.stack(where + [n_lane, n_block, 0, 0, 0]).astype(I32)

    w_rows = integrals.shape[1]
    flat = integrals.reshape(-1, 128)

    def run(n_lane, n_block, before):
        labels = (starts, irrep_first, irrep_second, irrep_target)
        return one_pass(position(n_lane, n_block), *labels, amplitudes, flat, w_rows, before)

    out = run(jnp.int32(0), jnp.int32(0), None)
    edges = jnp.arange(0, v, a_local, dtype=I32)
    low, high = starts[:8], starts[1:9]
    count = jnp.maximum(jnp.minimum(high, edges[:, None] + a_local) - jnp.maximum(low, edges[:, None]), 0)
    same = (jnp.arange(8)[:, None, None] ^ irrep_first[None, None, :]) == jnp.arange(8)[None, :, None]
    most = jnp.max(jnp.sum(count[:, None, :, None] * same[None].astype(I32), axis=(2, 3)))
    n_lanes = (most + LANES - 1) // LANES
    n_blocks = (jnp.max(high - low // 8 * 8) + BLOCK - 1) // BLOCK
    return lax.fori_loop(1, n_lanes * n_blocks, lambda n, acc: run(n % n_lanes, n // n_lanes, acc), out)


def solution(mesh):
    return jax.shard_map(
        per_device,
        mesh=mesh,
        in_specs=(P("depth", "col", "row"), P("depth", "row", "col", None), P(), P(), P(), P()),
        out_specs=P("col", "depth", "row"),
        check_vma=False,
    )
```

```python
import functools

import jax
import jax.numpy as jnp
from jax import lax
from jax.experimental import pallas as pl
from jax.experimental.pallas import tpu as pltpu
from jax.sharding import PartitionSpec as P


LANES = 512
BLOCK = 128
SMEM = pl.BlockSpec(memory_space=pltpu.SMEM)
VMEM = pl.BlockSpec(memory_space=pltpu.VMEM)
ANY = pl.BlockSpec(memory_space=pl.ANY)
F32, BF16, I32 = jnp.float32, jnp.bfloat16, jnp.int32


def label_of(place, starts):
    label = jnp.zeros_like(place)
    for irrep in range(1, 8):
        label = label + (place >= starts[irrep]).astype(I32)
    return label


def choose(index, scalars):
    out = jnp.full_like(index, scalars[0])
    for n in range(1, len(scalars)):
        out = jnp.where(index == n, scalars[n], out)
    return out


def two_terms(x):
    high = x.astype(BF16)
    return high, (x - high.astype(F32)).astype(BF16)


def nt(a, b):
    return lax.dot_general(a, b, (((1,), (1,)), ((), ())), preferred_element_type=F32)


def tn(a, b):
    return lax.dot_general(a, b, (((0,), (0,)), ((), ())), preferred_element_type=F32)


def x_places(pos, starts, first, x_local, oi):
    a_local = x_local // oi
    base = pos[0] * a_local
    x = lax.broadcasted_iota(I32, (1, x_local), 1)
    i = x % oi
    a = base + x // oi
    label = label_of(a, starts)
    firsts = [first[n] for n in range(oi)]
    s = label ^ choose(i, firsts)
    low = [jnp.maximum(starts[n], base) for n in range(8)]
    count = [jnp.maximum(jnp.minimum(starts[n + 1], base + a_local) - low[n], 0) for n in range(8)]
    place = a - choose(label, low)
    for n in range(oi - 1):
        place = place + jnp.where(n < i, choose(s ^ firsts[n], count), 0)
    return s, place - pos[3] * LANES


def pack_t_kernel(pos, starts, first, second, t_ref, out_ref, g_ref):
    k_local, c_local, x_local = t_ref.shape
    s, place = x_places(pos, starts, first, x_local, first.shape[0])
    c = pos[1] * c_local + lax.broadcasted_iota(I32, (c_local, 1), 0)
    label = label_of(c, starts)
    parts = []
    for k in range(k_local):
        keep = (label ^ second[pos[2] * k_local + k]) == s
        parts.extend(two_terms(jnp.where(keep, t_ref[k], 0.0)))
    stacked = jnp.concatenate(parts, 0)
    for n in range(LANES // 128):
        lanes = slice(n * 128, n * 128 + 128)
        rows = n * 128 + lax.broadcasted_iota(I32, (128, x_local), 0)
        hot = jnp.where(rows == place, 1.0, 0.0).astype(BF16)
        g_ref[lanes, :] = hot
        packed = nt(stacked, hot)
        for k in range(k_local):
            at = 2 * k * c_local
            out_ref[k, :, lanes] = packed[at : at + c_local] + packed[at + c_local : at + 2 * c_local]


def count_passes(starts, first, a_local, n_lanes, n_passes):
    lane = lax.broadcasted_iota(I32, (8, 128), 1)
    s, base = lane % 8, lane // 8 * a_local
    count = [
        jnp.maximum(jnp.minimum(starts[n + 1], base + a_local) - jnp.maximum(starts[n], base), 0) for n in range(8)
    ]
    places = jnp.zeros((8, 128), I32)
    for n in range(first.shape[0]):
        places = places + choose(s ^ first[n], count)
    most = jnp.max(jnp.where(lane < 32, places, 0).astype(F32)).astype(I32)
    widest = starts[1] - starts[0] // 8 * 8
    for n in range(1, 8):
        widest = jnp.maximum(widest, starts[n + 1] - starts[n] // 8 * 8)
    n_lanes[0] = (most + LANES - 1) // LANES
    n_passes[0] = (most + LANES - 1) // LANES * ((widest + BLOCK - 1) // BLOCK)


def pack_w_kernel(a_local, pos, starts, first, second, target, w_ref, out_ref, *limits):
    count_passes(starts, first, a_local, *limits)
    k_local, c_local, _ = out_ref.shape
    rows = k_local * c_local
    tiles = w_ref.shape[0] // rows
    row = lax.broadcasted_iota(I32, (c_local, 1), 0)
    label = label_of(pos[0] * c_local + row, starts) ^ target[pos[1]]
    wanted = jnp.concatenate([label ^ second[pos[2] * k_local + k] for k in range(k_local)], 0)
    firsts = [starts[n] // 8 * 8 for n in range(8)]
    total = jnp.zeros((2 * rows, BLOCK), F32)
    for q in range(tiles):
        b = q * 128 + lax.broadcasted_iota(I32, (1, 128), 1)
        label_b = label_of(b, starts)
        place = b - choose(label_b, firsts) - pos[4] * BLOCK
        hot = jnp.where(lax.broadcasted_iota(I32, (BLOCK, 128), 0) == place, 1.0, 0.0).astype(BF16)
        w = jnp.where(wanted == label_b, w_ref[pl.ds(q, rows, stride=tiles), :], 0.0)
        total = total + nt(jnp.concatenate(two_terms(w), 0), hot)
    for k in range(k_local):
        out_ref[k] = total[k * c_local : (k + 1) * c_local] + total[rows + k * c_local : rows + (k + 1) * c_local]


def three_terms(w, t):
    w_high, w_low = two_terms(w)
    t_high, t_low = two_terms(t)
    both = tn(jnp.concatenate([w_high, w_low], 1), t_high)
    return both[: w.shape[1]] + both[w.shape[1] :] + tn(w_high, t_low)


def put_window(pos, place, piece, into, k=None):
    size = piece.shape[1]
    core = 1 - pos[1] % 2 if place[1] else pos[1] % 2
    at = (lax.rem(pos[1] // 2 + place[0] + 8, 8) * 2 + core) * size
    rows = pl.ds(pl.multiple_of(at, 8), size)
    for n in range(piece.shape[0]):
        into[n if k is None else k, rows, :] = piece[n]


def place_kernel(where, pos, *refs):
    pieces, (own, pair, far), (t_all, w_all, total) = refs[: len(where)], refs[len(where) : -3], refs[-3:]
    for place, piece in zip(where, pieces):
        put_window(pos, place, piece, t_all)
    total[...] = jnp.zeros_like(total)
    size = own.shape[1]
    r = pos[0]
    for row, piece in ((r, own), (r ^ 1, pair), (3 - r, far.at[0]), ((3 - r) ^ 1, far.at[1])):
        for k in range(own.shape[0]):
            w_all[k, pl.ds(pl.multiple_of(row * size, 8), size), :] = piece[k]


def rows_for(pos, total, step, part):
    b_local = (total.shape[0] - BLOCK) // 4
    at = lax.rem(pos[2] + step, 4) * b_local + part * (b_local // 2)
    return total[pl.ds(pl.multiple_of(at, 8), b_local // 2), :]


def product_kernel(where, pos, starts, second, target, given, zeros, w_all, *refs):
    pieces, (t_all, total, up, down, one, three) = refs[: len(where)], refs[len(where) :]
    k_local, c_all, _ = t_all.shape
    for (k, place), piece in zip(where, pieces):
        put_window(pos, place, piece, t_all, k)
    row = lax.broadcasted_iota(I32, (128, 1), 0)

    def one_irrep(irrep, _):
        s = target[pos[1]] ^ irrep
        to = starts[irrep] // 8 * 8 + pos[4] * BLOCK
        spans = []
        for k in range(k_local):
            p = s ^ second[pos[2] * k_local + k]
            spans.append((starts[p], starts[p + 1], starts[p] // 8 * 8))
        trips = jnp.maximum(*[(end - aligned + 127) // 128 for _, end, aligned in spans])

        def step(n, _):
            w_rows, t_rows = [], []
            for k, (begin, end, aligned) in enumerate(spans):
                nominal = aligned + n * 128
                at = pl.multiple_of(jnp.minimum(nominal, c_all - 128), 8)
                c = at + row
                keep = (c >= jnp.maximum(begin, nominal)) & (c < end)
                w_rows.append(jnp.where(keep, w_all[k, pl.ds(at, 128), :], 0.0))
                t_rows.append(t_all[k, pl.ds(at, 128), :])
            term = three_terms(jnp.concatenate(w_rows, 0), jnp.concatenate(t_rows, 0))
            total[pl.ds(pl.multiple_of(to, 8), BLOCK), :] += term
            return 0

        return lax.fori_loop(0, jnp.where(to < starts[irrep + 1], trips, 0), step, 0)

    lax.fori_loop(0, 8, one_irrep, 0)
    for out, step, part in ((up, 2, 0), (down, 2, 1), (one, 1, 1), (three, 3, 0)):
        out[...] = rows_for(pos, total, step, part)


def join_kernel(pos, total, relay_up, relay_down, one, three):
    one[...] = rows_for(pos, total, 1, 0) + relay_up[...]
    three[...] = rows_for(pos, total, 3, 1) + relay_down[...]


def expand_kernel(pos, starts, first, target, g_ref, *refs):
    total, one_0, one_1, three_0, three_1 = refs[:5]
    out_ref, buffer, sems = refs[-3:]
    b_local = out_ref.shape[1]
    x_local, oi, width = out_ref.shape[2], first.shape[0], 256
    upper = rows_for(pos, total, 0, 0) + one_0[...] + three_0[...]
    lower = rows_for(pos, total, 0, 1) + one_1[...] + three_1[...]
    sums = jnp.concatenate(two_terms(jnp.concatenate([upper, lower], 0)), 0)
    b = pos[2] * b_local + lax.broadcasted_iota(I32, (b_local, 1), 0)
    wanted = label_of(b, starts) ^ target[pos[1]]

    def tile(n, _):
        x = n * width + lax.broadcasted_iota(I32, (1, width), 1)
        lanes = pl.ds(pl.multiple_of(n * width, width), width)
        a = pos[0] * (x_local // oi) + x // oi
        s = label_of(a, starts) ^ choose(x % oi, [first[i] for i in range(oi)])
        both = jnp.dot(sums, g_ref[:, lanes], preferred_element_type=F32)
        value = jnp.where(wanted == s, both[:b_local] + both[b_local:], 0.0)
        buffer[:, lanes] = value + refs[5][0, :, lanes] if len(refs) > 8 else value
        pltpu.make_async_copy(buffer.at[:, lanes], out_ref.at[0, :, lanes], sems.at[n]).start()
        return 0

    tiles = x_local // width
    lax.fori_loop(0, tiles, tile, 0)
    for n in range(tiles):
        lanes = pl.ds(n * width, width)
        pltpu.make_async_copy(buffer.at[:, lanes], out_ref.at[0, :, lanes], sems.at[n]).wait()


def params(mib=16):
    return pltpu.CompilerParams(vmem_limit_bytes=mib * 1024 * 1024)


def one_pass(pos, starts, first, second, target, amplitudes, integrals, w_rows, before):
    k_local, c_local, x_local = amplitudes.shape
    v = c_local * 16
    b_local = v // 4
    shape = jax.ShapeDtypeStruct
    t0, hot = pl.pallas_call(
        pack_t_kernel,
        out_shape=(shape((k_local, c_local, LANES), F32), shape((LANES, x_local), BF16)),
        in_specs=[SMEM] * 4 + [VMEM],
        out_specs=(VMEM,) * 2,
        compiler_params=params(),
        name="pack_t",
    )(pos, starts, first, second, amplitudes)
    w0, *limits = pl.pallas_call(
        functools.partial(pack_w_kernel, x_local // first.shape[0]),
        out_shape=(shape((k_local, w_rows, BLOCK), F32), shape((1,), I32), shape((1,), I32)),
        in_specs=[SMEM] * 5 + [VMEM],
        out_specs=(VMEM, SMEM, SMEM),
        compiler_params=params(),
        cost_estimate=pl.CostEstimate(flops=10**9, bytes_accessed=4 * 10**6, transcendentals=0),
        name="pack_w",
    )(pos, starts, first, second, target, integrals)

    def along(x, axis, step):
        return lax.ppermute(x, axis, [(i, (i + step) % 4) for i in range(4)])

    def swap(x):
        return lax.ppermute(x, "col", [(i, i ^ 1) for i in range(16)])

    def ring(x, step):
        return lax.ppermute(x, "col", [(i, (i + 2 * step) % 16) for i in range(16)])

    got = {(0, False): t0}
    right = left = t0
    for n in range(1, 4):
        right, left = ring(right, 1), ring(left, -1)
        got[-n, False], got[n, False] = right, left
    late = [ring(right[:1], 1), ring(left[1:], -1)]
    for (far, _), piece in list(got.items()):
        got[far, True] = swap(piece)
    pair = lax.ppermute(w0, "row", [(i, i ^ 1) for i in range(4)])
    far = lax.ppermute(jnp.stack([w0, pair]), "row", [(i, 3 - i) for i in range(4)])
    t_all, w_all, total = pl.pallas_call(
        functools.partial(place_kernel, list(got)),
        out_shape=(shape((k_local, v, LANES), F32), shape((k_local, v, BLOCK), F32), shape((v + BLOCK, LANES), F32)),
        in_specs=[SMEM] + [VMEM] * (len(got) + 3),
        out_specs=(VMEM,) * 3,
        compiler_params=params(),
        cost_estimate=pl.CostEstimate(flops=0, bytes_accessed=7 * 10**6, transcendentals=0),
        name="place",
    )(pos, *got.values(), w0, pair, far)
    late += [swap(piece) for piece in late]
    where = [(0, (4, False)), (1, (4, False)), (0, (4, True)), (1, (4, True))]
    part = shape((b_local // 2, LANES), F32)
    _, total, up, down, one_1, three_0 = pl.pallas_call(
        functools.partial(product_kernel, where),
        out_shape=(shape(t_all.shape, F32), shape(total.shape, F32)) + (part,) * 4,
        in_specs=[SMEM] * 4 + [VMEM] * 7,
        out_specs=(VMEM,) * 6,
        input_output_aliases={4: 0, 5: 1},
        compiler_params=params(),
        name="product",
    )(pos, starts, second, target, t_all, total, w_all, *late)
    up, down = along(up, "depth", 1), along(down, "depth", -1)
    one_1, three_0 = along(one_1, "depth", 1), along(three_0, "depth", -1)
    one_0, three_1 = pl.pallas_call(
        join_kernel,
        out_shape=(part,) * 2,
        in_specs=[SMEM] + [VMEM] * 3,
        out_specs=(VMEM,) * 2,
        compiler_params=params(4),
        name="join",
    )(pos, total, up, down)
    one_0, three_1 = along(one_0, "depth", 1), along(three_1, "depth", -1)
    sums = [total, one_0, one_1, three_0, three_1]
    more = [] if before is None else [before]
    out = pl.pallas_call(
        expand_kernel,
        out_shape=shape((1, b_local, x_local), F32),
        in_specs=[SMEM] * 4 + [VMEM] * (6 + len(more)),
        out_specs=ANY,
        scratch_shapes=[pltpu.VMEM((b_local, x_local), F32), pltpu.SemaphoreType.DMA((x_local // 256,))],
        compiler_params=params(),
        name="expand",
    )(pos, starts, first, target, hot, *sums, *more)
    return out, limits


def per_device(amplitudes, integrals, irrep_virtual, irrep_first, irrep_second, irrep_target):
    starts = jnp.sum((irrep_virtual[None, :] < jnp.arange(16, dtype=I32)[:, None]).astype(I32), axis=1)
    where = [lax.axis_index(n).astype(I32) for n in ("row", "col", "depth")]

    def position(n_lane, n_block):
        return jnp.stack(where + [n_lane, n_block, 0, 0, 0]).astype(I32)

    w_rows = integrals.shape[1]
    flat = integrals.reshape(-1, 128)

    def run(n_lane, n_block, before):
        labels = (starts, irrep_first, irrep_second, irrep_target)
        return one_pass(position(n_lane, n_block), *labels, amplitudes, flat, w_rows, before)

    out, limits = run(jnp.int32(0), jnp.int32(0), None)
    n_lanes, n_passes = (limit.reshape(()) for limit in limits)
    return lax.fori_loop(1, n_passes, lambda n, acc: run(n % n_lanes, n // n_lanes, acc)[0], out)


def solution(mesh):
    return jax.shard_map(
        per_device,
        mesh=mesh,
        in_specs=(P("depth", "col", "row"), P("depth", "row", "col", None), P(), P(), P(), P()),
        out_specs=P("col", "depth", "row"),
        check_vma=False,
    )
```

```python
import functools

import jax
import jax.numpy as jnp
from jax import lax
from jax.experimental import pallas as pl
from jax.experimental.pallas import tpu as pltpu
from jax.sharding import PartitionSpec as P


LANES = 512
BLOCK = 128
SMEM = pl.BlockSpec(memory_space=pltpu.SMEM)
VMEM = pl.BlockSpec(memory_space=pltpu.VMEM)
ANY = pl.BlockSpec(memory_space=pl.ANY)
F32, BF16, I32 = jnp.float32, jnp.bfloat16, jnp.int32


def label_of(place, starts):
    label = jnp.zeros_like(place)
    for irrep in range(1, 8):
        label = label + (place >= starts[irrep]).astype(I32)
    return label


def choose(index, scalars):
    out = jnp.full_like(index, scalars[0])
    for n in range(1, len(scalars)):
        out = jnp.where(index == n, scalars[n], out)
    return out


def two_terms(x):
    high = x.astype(BF16)
    return high, (x - high.astype(F32)).astype(BF16)


def nt(a, b):
    return lax.dot_general(a, b, (((1,), (1,)), ((), ())), preferred_element_type=F32)


def tn(a, b):
    return lax.dot_general(a, b, (((0,), (0,)), ((), ())), preferred_element_type=F32)


def x_places(pos, starts, first, x_local, oi):
    a_local = x_local // oi
    base = pos[0] * a_local
    x = lax.broadcasted_iota(I32, (1, x_local), 1)
    i = x % oi
    a = base + x // oi
    label = label_of(a, starts)
    firsts = [first[n] for n in range(oi)]
    s = label ^ choose(i, firsts)
    low = [jnp.maximum(starts[n], base) for n in range(8)]
    count = [jnp.maximum(jnp.minimum(starts[n + 1], base + a_local) - low[n], 0) for n in range(8)]
    place = a - choose(label, low)
    for n in range(oi - 1):
        place = place + jnp.where(n < i, choose(s ^ firsts[n], count), 0)
    return s, place - pos[3] * LANES


def pack_t_kernel(pos, starts, first, second, t_ref, out_ref, g_ref):
    k_local, c_local, x_local = t_ref.shape
    s, place = x_places(pos, starts, first, x_local, first.shape[0])
    c = pos[1] * c_local + lax.broadcasted_iota(I32, (c_local, 1), 0)
    label = label_of(c, starts)
    parts = []
    for k in range(k_local):
        keep = (label ^ second[pos[2] * k_local + k]) == s
        parts.extend(two_terms(jnp.where(keep, t_ref[k], 0.0)))
    stacked = jnp.concatenate(parts, 0)
    for n in range(LANES // 128):
        lanes = slice(n * 128, n * 128 + 128)
        rows = n * 128 + lax.broadcasted_iota(I32, (128, x_local), 0)
        hot = jnp.where(rows == place, 1.0, 0.0).astype(BF16)
        g_ref[lanes, :] = hot
        packed = nt(stacked, hot)
        for k in range(k_local):
            at = 2 * k * c_local
            out_ref[k, :, lanes] = packed[at : at + c_local] + packed[at + c_local : at + 2 * c_local]


def count_passes(starts, first, a_local, n_lanes, n_passes):
    lane = lax.broadcasted_iota(I32, (8, 128), 1)
    s, base = lane % 8, lane // 8 * a_local
    count = [
        jnp.maximum(jnp.minimum(starts[n + 1], base + a_local) - jnp.maximum(starts[n], base), 0) for n in range(8)
    ]
    places = jnp.zeros((8, 128), I32)
    for n in range(first.shape[0]):
        places = places + choose(s ^ first[n], count)
    most = jnp.max(jnp.where(lane < 32, places, 0).astype(F32)).astype(I32)
    widest = starts[1] - starts[0] // 8 * 8
    for n in range(1, 8):
        widest = jnp.maximum(widest, starts[n + 1] - starts[n] // 8 * 8)
    n_lanes[0] = (most + LANES - 1) // LANES
    n_passes[0] = (most + LANES - 1) // LANES * ((widest + BLOCK - 1) // BLOCK)


def pack_w_kernel(a_local, pos, starts, first, second, target, w_ref, out_ref, *limits):
    count_passes(starts, first, a_local, *limits)
    k_local, c_local, _ = out_ref.shape
    rows = k_local * c_local
    tiles = w_ref.shape[0] // rows
    row = lax.broadcasted_iota(I32, (c_local, 1), 0)
    label = label_of(pos[0] * c_local + row, starts) ^ target[pos[1]]
    wanted = jnp.concatenate([label ^ second[pos[2] * k_local + k] for k in range(k_local)], 0)
    firsts = [starts[n] // 8 * 8 for n in range(8)]
    total = jnp.zeros((2 * rows, BLOCK), F32)
    for q in range(tiles):
        b = q * 128 + lax.broadcasted_iota(I32, (1, 128), 1)
        label_b = label_of(b, starts)
        place = b - choose(label_b, firsts) - pos[4] * BLOCK
        hot = jnp.where(lax.broadcasted_iota(I32, (BLOCK, 128), 0) == place, 1.0, 0.0).astype(BF16)
        w = jnp.where(wanted == label_b, w_ref[pl.ds(q, rows, stride=tiles), :], 0.0)
        total = total + nt(jnp.concatenate(two_terms(w), 0), hot)
    for k in range(k_local):
        out_ref[k] = total[k * c_local : (k + 1) * c_local] + total[rows + k * c_local : rows + (k + 1) * c_local]


def three_terms(w, t):
    w_high, w_low = two_terms(w)
    t_high, t_low = two_terms(t)
    both = tn(jnp.concatenate([w_high, w_low], 1), t_high)
    return both[: w.shape[1]] + both[w.shape[1] :] + tn(w_high, t_low)


def put_window(pos, place, piece, into, k=None):
    size = piece.shape[1]
    core = 1 - pos[1] % 2 if place[1] else pos[1] % 2
    at = (lax.rem(pos[1] // 2 + place[0] + 8, 8) * 2 + core) * size
    rows = pl.ds(pl.multiple_of(at, 8), size)
    for n in range(piece.shape[0]):
        into[n if k is None else k, rows, :] = piece[n]


def place_kernel(where, pos, *refs):
    pieces, (own, pair, far), (t_all, w_all, total) = refs[: len(where)], refs[len(where) : -3], refs[-3:]
    for place, piece in zip(where, pieces):
        put_window(pos, place, piece, t_all)
    total[...] = jnp.zeros_like(total)
    size = own.shape[1]
    r = pos[0]
    for row, piece in ((r, own), (r ^ 1, pair), (3 - r, far.at[0]), ((3 - r) ^ 1, far.at[1])):
        for k in range(own.shape[0]):
            w_all[k, pl.ds(pl.multiple_of(row * size, 8), size), :] = piece[k]


def rows_for(pos, total, step, part):
    b_local = (total.shape[0] - BLOCK) // 4
    at = lax.rem(pos[2] + step, 4) * b_local + part * (b_local // 2)
    return total[pl.ds(pl.multiple_of(at, 8), b_local // 2), :]


def product_kernel(where, pos, starts, second, target, given, zeros, w_all, *refs):
    pieces, (t_all, total, up, down, one, three) = refs[: len(where)], refs[len(where) :]
    k_local, c_all, _ = t_all.shape
    for (k, place), piece in zip(where, pieces):
        put_window(pos, place, piece, t_all, k)
    row = lax.broadcasted_iota(I32, (128, 1), 0)

    def one_irrep(irrep, _):
        s = target[pos[1]] ^ irrep
        to = starts[irrep] // 8 * 8 + pos[4] * BLOCK
        spans = []
        for k in range(k_local):
            p = s ^ second[pos[2] * k_local + k]
            spans.append((starts[p], starts[p + 1], starts[p] // 8 * 8))
        trips = jnp.maximum(*[(end - aligned + 127) // 128 for _, end, aligned in spans])

        def step(n, _):
            w_rows, t_rows = [], []
            for k, (begin, end, aligned) in enumerate(spans):
                nominal = aligned + n * 128
                at = pl.multiple_of(jnp.minimum(nominal, c_all - 128), 8)
                c = at + row
                keep = (c >= jnp.maximum(begin, nominal)) & (c < end)
                w_rows.append(jnp.where(keep, w_all[k, pl.ds(at, 128), :], 0.0))
                t_rows.append(t_all[k, pl.ds(at, 128), :])
            term = three_terms(jnp.concatenate(w_rows, 0), jnp.concatenate(t_rows, 0))
            total[pl.ds(pl.multiple_of(to, 8), BLOCK), :] += term
            return 0

        return lax.fori_loop(0, jnp.where(to < starts[irrep + 1], trips, 0), step, 0)

    lax.fori_loop(0, 8, one_irrep, 0)
    for out, step, part in ((up, 2, 0), (down, 2, 1), (one, 1, 1), (three, 3, 0)):
        out[...] = rows_for(pos, total, step, part)


def join_kernel(pos, total, relay_up, relay_down, one, three):
    one[...] = rows_for(pos, total, 1, 0) + relay_up[...]
    three[...] = rows_for(pos, total, 3, 1) + relay_down[...]


def expand_kernel(pos, starts, first, target, g_ref, *refs):
    total, one_0, one_1, three_0, three_1 = refs[:5]
    out_ref, buffer, sems = refs[-3:]
    b_local = out_ref.shape[1]
    x_local, oi, width = out_ref.shape[2], first.shape[0], 256
    upper = rows_for(pos, total, 0, 0) + one_0[...] + three_0[...]
    lower = rows_for(pos, total, 0, 1) + one_1[...] + three_1[...]
    sums = jnp.concatenate(two_terms(jnp.concatenate([upper, lower], 0)), 0)
    b = pos[2] * b_local + lax.broadcasted_iota(I32, (b_local, 1), 0)
    wanted = label_of(b, starts) ^ target[pos[1]]

    def tile(n, _):
        x = n * width + lax.broadcasted_iota(I32, (1, width), 1)
        lanes = pl.ds(pl.multiple_of(n * width, width), width)
        a = pos[0] * (x_local // oi) + x // oi
        s = label_of(a, starts) ^ choose(x % oi, [first[i] for i in range(oi)])
        both = jnp.dot(sums, g_ref[:, lanes], preferred_element_type=F32)
        value = jnp.where(wanted == s, both[:b_local] + both[b_local:], 0.0)
        buffer[:, lanes] = value + refs[5][0, :, lanes] if len(refs) > 8 else value
        pltpu.make_async_copy(buffer.at[:, lanes], out_ref.at[0, :, lanes], sems.at[n]).start()
        return 0

    tiles = x_local // width
    lax.fori_loop(0, tiles, tile, 0)
    for n in range(tiles):
        lanes = pl.ds(n * width, width)
        pltpu.make_async_copy(buffer.at[:, lanes], out_ref.at[0, :, lanes], sems.at[n]).wait()


def params(mib=16):
    return pltpu.CompilerParams(vmem_limit_bytes=mib * 1024 * 1024)


def one_pass(pos, starts, first, second, target, amplitudes, integrals, w_rows, before):
    k_local, c_local, x_local = amplitudes.shape
    v = c_local * 16
    b_local = v // 4
    shape = jax.ShapeDtypeStruct
    t0, hot = pl.pallas_call(
        pack_t_kernel,
        out_shape=(shape((k_local, c_local, LANES), F32), shape((LANES, x_local), BF16)),
        in_specs=[SMEM] * 4 + [VMEM],
        out_specs=(VMEM,) * 2,
        compiler_params=params(),
        name="pack_t",
    )(pos, starts, first, second, amplitudes)
    w0, *limits = pl.pallas_call(
        functools.partial(pack_w_kernel, x_local // first.shape[0]),
        out_shape=(shape((k_local, w_rows, BLOCK), F32), shape((1,), I32), shape((1,), I32)),
        in_specs=[SMEM] * 5 + [VMEM],
        out_specs=(VMEM, SMEM, SMEM),
        compiler_params=params(),
        cost_estimate=pl.CostEstimate(flops=10**9, bytes_accessed=4 * 10**6, transcendentals=0),
        name="pack_w",
    )(pos, starts, first, second, target, integrals)

    n_lanes, n_passes = (limit.reshape(()) for limit in limits)
    passes = (n_lanes, n_passes, jnp.minimum(n_passes, 1), n_passes > 1)
    w0, passes = lax.optimization_barrier((w0, passes))

    def along(x, axis, step):
        return lax.ppermute(x, axis, [(i, (i + step) % 4) for i in range(4)])

    def swap(x):
        return lax.ppermute(x, "col", [(i, i ^ 1) for i in range(16)])

    def ring(x, step):
        return lax.ppermute(x, "col", [(i, (i + 2 * step) % 16) for i in range(16)])

    got = {(0, False): t0}
    right = left = t0
    for n in range(1, 4):
        right, left = ring(right, 1), ring(left, -1)
        got[-n, False], got[n, False] = right, left
    late = [ring(right[:1], 1), ring(left[1:], -1)]
    for (far, _), piece in list(got.items()):
        got[far, True] = swap(piece)
    pair = lax.ppermute(w0, "row", [(i, i ^ 1) for i in range(4)])
    far = lax.ppermute(jnp.stack([w0, pair]), "row", [(i, 3 - i) for i in range(4)])
    t_all, w_all, total = pl.pallas_call(
        functools.partial(place_kernel, list(got)),
        out_shape=(shape((k_local, v, LANES), F32), shape((k_local, v, BLOCK), F32), shape((v + BLOCK, LANES), F32)),
        in_specs=[SMEM] + [VMEM] * (len(got) + 3),
        out_specs=(VMEM,) * 3,
        compiler_params=params(),
        cost_estimate=pl.CostEstimate(flops=0, bytes_accessed=7 * 10**6, transcendentals=0),
        name="place",
    )(pos, *got.values(), w0, pair, far)
    late += [swap(piece) for piece in late]
    where = [(0, (4, False)), (1, (4, False)), (0, (4, True)), (1, (4, True))]
    part = shape((b_local // 2, LANES), F32)
    _, total, up, down, one_1, three_0 = pl.pallas_call(
        functools.partial(product_kernel, where),
        out_shape=(shape(t_all.shape, F32), shape(total.shape, F32)) + (part,) * 4,
        in_specs=[SMEM] * 4 + [VMEM] * 7,
        out_specs=(VMEM,) * 6,
        input_output_aliases={4: 0, 5: 1},
        compiler_params=params(),
        name="product",
    )(pos, starts, second, target, t_all, total, w_all, *late)
    up, down = along(up, "depth", 1), along(down, "depth", -1)
    one_1, three_0 = along(one_1, "depth", 1), along(three_0, "depth", -1)
    one_0, three_1 = pl.pallas_call(
        join_kernel,
        out_shape=(part,) * 2,
        in_specs=[SMEM] + [VMEM] * 3,
        out_specs=(VMEM,) * 2,
        compiler_params=params(4),
        name="join",
    )(pos, total, up, down)
    one_0, three_1 = along(one_0, "depth", 1), along(three_1, "depth", -1)
    sums = [total, one_0, one_1, three_0, three_1]
    more = [] if before is None else [before]
    out = pl.pallas_call(
        expand_kernel,
        out_shape=shape((1, b_local, x_local), F32),
        in_specs=[SMEM] * 4 + [VMEM] * (6 + len(more)),
        out_specs=ANY,
        scratch_shapes=[pltpu.VMEM((b_local, x_local), F32), pltpu.SemaphoreType.DMA((x_local // 256,))],
        compiler_params=params(),
        name="expand",
    )(pos, starts, first, target, hot, *sums, *more)
    return out, passes


def per_device(amplitudes, integrals, irrep_virtual, irrep_first, irrep_second, irrep_target):
    starts = jnp.sum((irrep_virtual[None, :] < jnp.arange(16, dtype=I32)[:, None]).astype(I32), axis=1)
    where = [lax.axis_index(n).astype(I32) for n in ("row", "col", "depth")]

    def position(n_lane, n_block):
        return jnp.stack(where + [n_lane, n_block, 0, 0, 0]).astype(I32)

    w_rows = integrals.shape[1]
    flat = integrals.reshape(-1, 128)

    def run(n_lane, n_block, before):
        labels = (starts, irrep_first, irrep_second, irrep_target)
        return one_pass(position(n_lane, n_block), *labels, amplitudes, flat, w_rows, before)

    out, (n_lanes, n_passes, done, more) = run(jnp.int32(0), jnp.int32(0), None)

    def further(state):
        n, _, acc = state
        return n + 1, n + 1 < n_passes, run(lax.rem(n, n_lanes), lax.div(n, n_lanes), acc)[0]

    return lax.while_loop(lambda state: state[1], further, (done, more, out))[2]


def solution(mesh):
    return jax.shard_map(
        per_device,
        mesh=mesh,
        in_specs=(P("depth", "col", "row"), P("depth", "row", "col", None), P(), P(), P(), P()),
        out_specs=P("col", "depth", "row"),
        check_vma=False,
    )
```

```python
import functools

import jax
import jax.numpy as jnp
from jax import lax
from jax.experimental import pallas as pl
from jax.experimental.pallas import tpu as pltpu
from jax.sharding import PartitionSpec as P


LANES = 512
BLOCK = 128
SMEM = pl.BlockSpec(memory_space=pltpu.SMEM)
VMEM = pl.BlockSpec(memory_space=pltpu.VMEM)
ANY = pl.BlockSpec(memory_space=pl.ANY)
F32, BF16, I32 = jnp.float32, jnp.bfloat16, jnp.int32


def label_of(place, starts):
    label = jnp.zeros_like(place)
    for irrep in range(1, 8):
        label = label + (place >= starts[irrep]).astype(I32)
    return label


def choose(index, scalars):
    out = jnp.full_like(index, scalars[0])
    for n in range(1, len(scalars)):
        out = jnp.where(index == n, scalars[n], out)
    return out


def two_terms(x):
    high = x.astype(BF16)
    return high, (x - high.astype(F32)).astype(BF16)


def nt(a, b):
    return lax.dot_general(a, b, (((1,), (1,)), ((), ())), preferred_element_type=F32)


def tn(a, b):
    return lax.dot_general(a, b, (((0,), (0,)), ((), ())), preferred_element_type=F32)


def x_places(pos, starts, first, x_local, oi):
    a_local = x_local // oi
    base = pos[0] * a_local
    x = lax.broadcasted_iota(I32, (1, x_local), 1)
    i = x % oi
    a = base + x // oi
    label = label_of(a, starts)
    firsts = [first[n] for n in range(oi)]
    s = label ^ choose(i, firsts)
    low = [jnp.maximum(starts[n], base) for n in range(8)]
    count = [jnp.maximum(jnp.minimum(starts[n + 1], base + a_local) - low[n], 0) for n in range(8)]
    place = a - choose(label, low)
    for n in range(oi - 1):
        place = place + jnp.where(n < i, choose(s ^ firsts[n], count), 0)
    return s, place - pos[3] * LANES


def pack_t_kernel(pos, starts, first, second, t_ref, out_ref, g_ref):
    k_local, c_local, x_local = t_ref.shape
    s, place = x_places(pos, starts, first, x_local, first.shape[0])
    c = pos[1] * c_local + lax.broadcasted_iota(I32, (c_local, 1), 0)
    label = label_of(c, starts)
    parts = []
    for k in range(k_local):
        keep = (label ^ second[pos[2] * k_local + k]) == s
        parts.extend(two_terms(jnp.where(keep, t_ref[k], 0.0)))
    stacked = jnp.concatenate(parts, 0)
    width = 256
    for n in range(LANES // width):
        lanes = slice(n * width, n * width + width)
        rows = n * width + lax.broadcasted_iota(I32, (width, x_local), 0)
        hot = jnp.where(rows == place, 1.0, 0.0).astype(BF16)
        g_ref[lanes, :] = hot
        packed = nt(stacked, hot)
        for k in range(k_local):
            at = 2 * k * c_local
            out_ref[k, :, lanes] = packed[at : at + c_local] + packed[at + c_local : at + 2 * c_local]


def count_passes(starts, first, a_local, n_lanes, n_passes):
    lane = lax.broadcasted_iota(I32, (8, 128), 1)
    s, base = lane % 8, lane // 8 * a_local
    count = [
        jnp.maximum(jnp.minimum(starts[n + 1], base + a_local) - jnp.maximum(starts[n], base), 0) for n in range(8)
    ]
    places = jnp.zeros((8, 128), I32)
    for n in range(first.shape[0]):
        places = places + choose(s ^ first[n], count)
    most = jnp.max(jnp.where(lane < 32, places, 0).astype(F32)).astype(I32)
    widest = starts[1] - starts[0] // 8 * 8
    for n in range(1, 8):
        widest = jnp.maximum(widest, starts[n + 1] - starts[n] // 8 * 8)
    n_lanes[0] = (most + LANES - 1) // LANES
    n_passes[0] = (most + LANES - 1) // LANES * ((widest + BLOCK - 1) // BLOCK)


def pack_w_kernel(a_local, pos, starts, first, second, target, w_ref, out_ref, *limits):
    count_passes(starts, first, a_local, *limits)
    k_local, c_local, _ = out_ref.shape
    rows = k_local * c_local
    tiles = w_ref.shape[0] // rows
    row = lax.broadcasted_iota(I32, (c_local, 1), 0)
    label = label_of(pos[0] * c_local + row, starts) ^ target[pos[1]]
    wanted = jnp.concatenate([label ^ second[pos[2] * k_local + k] for k in range(k_local)], 0)
    firsts = [starts[n] // 8 * 8 for n in range(8)]
    total = jnp.zeros((2 * rows, BLOCK), F32)
    for q in range(tiles):
        b = q * 128 + lax.broadcasted_iota(I32, (1, 128), 1)
        label_b = label_of(b, starts)
        place = b - choose(label_b, firsts) - pos[4] * BLOCK
        hot = jnp.where(lax.broadcasted_iota(I32, (BLOCK, 128), 0) == place, 1.0, 0.0).astype(BF16)
        w = jnp.where(wanted == label_b, w_ref[pl.ds(q, rows, stride=tiles), :], 0.0)
        total = total + nt(jnp.concatenate(two_terms(w), 0), hot)
    for k in range(k_local):
        out_ref[k] = total[k * c_local : (k + 1) * c_local] + total[rows + k * c_local : rows + (k + 1) * c_local]


def three_terms(w, t):
    w_high, w_low = two_terms(w)
    t_high, t_low = two_terms(t)
    both = tn(jnp.concatenate([w_high, w_low], 1), t_high)
    return both[: w.shape[1]] + both[w.shape[1] :] + tn(w_high, t_low)


def put_window(pos, place, piece, into, k=None):
    size = piece.shape[1]
    core = 1 - pos[1] % 2 if place[1] else pos[1] % 2
    at = (lax.rem(pos[1] // 2 + place[0] + 8, 8) * 2 + core) * size
    rows = pl.ds(pl.multiple_of(at, 8), size)
    for n in range(piece.shape[0]):
        into[n if k is None else k, rows, :] = piece[n]


def place_kernel(where, pos, *refs):
    pieces, (own, pair, far), (t_all, w_all, total) = refs[: len(where)], refs[len(where) : -3], refs[-3:]
    for place, piece in zip(where, pieces):
        put_window(pos, place, piece, t_all)
    total[...] = jnp.zeros_like(total)
    size = own.shape[1]
    r = pos[0]
    for row, piece in ((r, own), (r ^ 1, pair), (3 - r, far.at[0]), ((3 - r) ^ 1, far.at[1])):
        for k in range(own.shape[0]):
            w_all[k, pl.ds(pl.multiple_of(row * size, 8), size), :] = piece[k]


def rows_for(pos, total, step, part):
    b_local = (total.shape[0] - BLOCK) // 4
    at = lax.rem(pos[2] + step, 4) * b_local + part * (b_local // 2)
    return total[pl.ds(pl.multiple_of(at, 8), b_local // 2), :]


def product_kernel(where, pos, starts, second, target, given, zeros, w_all, *refs):
    pieces, (t_all, total, up, down, one, three) = refs[: len(where)], refs[len(where) :]
    k_local, c_all, _ = t_all.shape
    for (k, place), piece in zip(where, pieces):
        put_window(pos, place, piece, t_all, k)
    row = lax.broadcasted_iota(I32, (128, 1), 0)

    def one_irrep(irrep, _):
        s = target[pos[1]] ^ irrep
        to = starts[irrep] // 8 * 8 + pos[4] * BLOCK
        spans = []
        for k in range(k_local):
            p = s ^ second[pos[2] * k_local + k]
            spans.append((starts[p], starts[p + 1], starts[p] // 8 * 8))
        trips = jnp.maximum(*[(end - aligned + 127) // 128 for _, end, aligned in spans])

        def step(n, _):
            w_rows, t_rows = [], []
            for k, (begin, end, aligned) in enumerate(spans):
                nominal = aligned + n * 128
                at = pl.multiple_of(jnp.minimum(nominal, c_all - 128), 8)
                c = at + row
                keep = (c >= jnp.maximum(begin, nominal)) & (c < end)
                w_rows.append(jnp.where(keep, w_all[k, pl.ds(at, 128), :], 0.0))
                t_rows.append(t_all[k, pl.ds(at, 128), :])
            term = three_terms(jnp.concatenate(w_rows, 0), jnp.concatenate(t_rows, 0))
            total[pl.ds(pl.multiple_of(to, 8), BLOCK), :] += term
            return 0

        return lax.fori_loop(0, jnp.where(to < starts[irrep + 1], trips, 0), step, 0)

    lax.fori_loop(0, 8, one_irrep, 0)
    for out, step, part in ((up, 2, 0), (down, 2, 1), (one, 1, 1), (three, 3, 0)):
        out[...] = rows_for(pos, total, step, part)


def join_kernel(pos, total, relay_up, relay_down, one, three):
    one[...] = rows_for(pos, total, 1, 0) + relay_up[...]
    three[...] = rows_for(pos, total, 3, 1) + relay_down[...]


def expand_kernel(pos, starts, first, target, g_ref, *refs):
    total, one_0, one_1, three_0, three_1 = refs[:5]
    out_ref, buffer, sems = refs[-3:]
    b_local = out_ref.shape[1]
    x_local, oi, width = out_ref.shape[2], first.shape[0], 256
    upper = rows_for(pos, total, 0, 0) + one_0[...] + three_0[...]
    lower = rows_for(pos, total, 0, 1) + one_1[...] + three_1[...]
    sums = jnp.concatenate(two_terms(jnp.concatenate([upper, lower], 0)), 0)
    b = pos[2] * b_local + lax.broadcasted_iota(I32, (b_local, 1), 0)
    wanted = label_of(b, starts) ^ target[pos[1]]

    def tile(n, _):
        x = n * width + lax.broadcasted_iota(I32, (1, width), 1)
        lanes = pl.ds(pl.multiple_of(n * width, width), width)
        a = pos[0] * (x_local // oi) + x // oi
        s = label_of(a, starts) ^ choose(x % oi, [first[i] for i in range(oi)])
        both = jnp.dot(sums, g_ref[:, lanes], preferred_element_type=F32)
        value = jnp.where(wanted == s, both[:b_local] + both[b_local:], 0.0)
        buffer[:, lanes] = value + refs[5][0, :, lanes] if len(refs) > 8 else value
        pltpu.make_async_copy(buffer.at[:, lanes], out_ref.at[0, :, lanes], sems.at[n]).start()
        return 0

    tiles = x_local // width
    lax.fori_loop(0, tiles, tile, 0)
    for n in range(tiles):
        lanes = pl.ds(n * width, width)
        pltpu.make_async_copy(buffer.at[:, lanes], out_ref.at[0, :, lanes], sems.at[n]).wait()


def params(mib=16):
    return pltpu.CompilerParams(vmem_limit_bytes=mib * 1024 * 1024)


def one_pass(pos, starts, first, second, target, amplitudes, integrals, w_rows, before):
    k_local, c_local, x_local = amplitudes.shape
    v = c_local * 16
    b_local = v // 4
    shape = jax.ShapeDtypeStruct
    t0, hot = pl.pallas_call(
        pack_t_kernel,
        out_shape=(shape((k_local, c_local, LANES), F32), shape((LANES, x_local), BF16)),
        in_specs=[SMEM] * 4 + [VMEM],
        out_specs=(VMEM,) * 2,
        compiler_params=params(),
        name="pack_t",
    )(pos, starts, first, second, amplitudes)
    w0, *limits = pl.pallas_call(
        functools.partial(pack_w_kernel, x_local // first.shape[0]),
        out_shape=(shape((k_local, w_rows, BLOCK), F32), shape((1,), I32), shape((1,), I32)),
        in_specs=[SMEM] * 5 + [VMEM],
        out_specs=(VMEM, SMEM, SMEM),
        compiler_params=params(),
        cost_estimate=pl.CostEstimate(flops=10**9, bytes_accessed=4 * 10**6, transcendentals=0),
        name="pack_w",
    )(pos, starts, first, second, target, integrals)

    n_lanes, n_passes = (limit.reshape(()) for limit in limits)
    passes = (n_lanes, n_passes, jnp.minimum(n_passes, 1), n_passes > 1)

    def along(x, axis, step):
        return lax.ppermute(x, axis, [(i, (i + step) % 4) for i in range(4)])

    def swap(x):
        return lax.ppermute(x, "col", [(i, i ^ 1) for i in range(16)])

    def ring(x, step):
        return lax.ppermute(x, "col", [(i, (i + 2 * step) % 16) for i in range(16)])

    got = {(0, False): t0}
    right = left = t0
    for n in range(1, 4):
        right, left = ring(right, 1), ring(left, -1)
        got[-n, False], got[n, False] = right, left
    late = [ring(right[:1], 1), ring(left[1:], -1)]
    for (far, _), piece in list(got.items()):
        got[far, True] = swap(piece)
    pair = lax.ppermute(w0, "row", [(i, i ^ 1) for i in range(4)])
    pair, passes = lax.optimization_barrier((pair, passes))
    far = lax.ppermute(jnp.stack([w0, pair]), "row", [(i, 3 - i) for i in range(4)])
    t_all, w_all, total = pl.pallas_call(
        functools.partial(place_kernel, list(got)),
        out_shape=(shape((k_local, v, LANES), F32), shape((k_local, v, BLOCK), F32), shape((v + BLOCK, LANES), F32)),
        in_specs=[SMEM] + [VMEM] * (len(got) + 3),
        out_specs=(VMEM,) * 3,
        compiler_params=params(),
        cost_estimate=pl.CostEstimate(flops=0, bytes_accessed=7 * 10**6, transcendentals=0),
        name="place",
    )(pos, *got.values(), w0, pair, far)
    late += [swap(piece) for piece in late]
    where = [(0, (4, False)), (1, (4, False)), (0, (4, True)), (1, (4, True))]
    part = shape((b_local // 2, LANES), F32)
    _, total, up, down, one_1, three_0 = pl.pallas_call(
        functools.partial(product_kernel, where),
        out_shape=(shape(t_all.shape, F32), shape(total.shape, F32)) + (part,) * 4,
        in_specs=[SMEM] * 4 + [VMEM] * 7,
        out_specs=(VMEM,) * 6,
        input_output_aliases={4: 0, 5: 1},
        compiler_params=params(),
        name="product",
    )(pos, starts, second, target, t_all, total, w_all, *late)
    up, down = along(up, "depth", 1), along(down, "depth", -1)
    one_1, three_0 = along(one_1, "depth", 1), along(three_0, "depth", -1)
    one_0, three_1 = pl.pallas_call(
        join_kernel,
        out_shape=(part,) * 2,
        in_specs=[SMEM] + [VMEM] * 3,
        out_specs=(VMEM,) * 2,
        compiler_params=params(4),
        name="join",
    )(pos, total, up, down)
    one_0, three_1 = along(one_0, "depth", 1), along(three_1, "depth", -1)
    sums = [total, one_0, one_1, three_0, three_1]
    more = [] if before is None else [before]
    out = pl.pallas_call(
        expand_kernel,
        out_shape=shape((1, b_local, x_local), F32),
        in_specs=[SMEM] * 4 + [VMEM] * (6 + len(more)),
        out_specs=ANY,
        scratch_shapes=[pltpu.VMEM((b_local, x_local), F32), pltpu.SemaphoreType.DMA((x_local // 256,))],
        compiler_params=params(),
        name="expand",
    )(pos, starts, first, target, hot, *sums, *more)
    return out, passes


def per_device(amplitudes, integrals, irrep_virtual, irrep_first, irrep_second, irrep_target):
    starts = jnp.sum((irrep_virtual[None, :] < jnp.arange(16, dtype=I32)[:, None]).astype(I32), axis=1)
    where = [lax.axis_index(n).astype(I32) for n in ("row", "col", "depth")]

    def position(n_lane, n_block):
        return jnp.stack(where + [n_lane, n_block, 0, 0, 0]).astype(I32)

    w_rows = integrals.shape[1]
    flat = integrals.reshape(-1, 128)

    def run(n_lane, n_block, before):
        labels = (starts, irrep_first, irrep_second, irrep_target)
        return one_pass(position(n_lane, n_block), *labels, amplitudes, flat, w_rows, before)

    out, (n_lanes, n_passes, done, more) = run(jnp.int32(0), jnp.int32(0), None)

    def further(state):
        n, _, acc = state
        return n + 1, n + 1 < n_passes, run(lax.rem(n, n_lanes), lax.div(n, n_lanes), acc)[0]

    return lax.while_loop(lambda state: state[1], further, (done, more, out))[2]


def solution(mesh):
    return jax.shard_map(
        per_device,
        mesh=mesh,
        in_specs=(P("depth", "col", "row"), P("depth", "row", "col", None), P(), P(), P(), P()),
        out_specs=P("col", "depth", "row"),
        check_vma=False,
    )
```
